128 devices in a mesh: wall: 4 (over x), drops: 32 (over y, z, core).
Axes of the slice: x: 4, y: 4, z: 4, core: 2. Of those that a mesh axis runs over, the one named last changes fastest.
Arguments:
- drop_points: float32 [1024, 3, 544], P(('wall', 'drops')), may hold values from -6 to 6
- drop_strength: float32 [1024, 3, 544], P(('wall', 'drops')), may hold values from -0.25 to 0.25
- upsample: float32 [544, 2112], replicated, may hold values from -0.25 to 0.25
- base_velocity: float32 [1024, 3, 544], P(('wall', 'drops')), may hold values from -6 to 6
- near_drops: int32 [1024, 4], P(('wall', 'drops')), may hold values from 0 to 1023, as said below
- near_count: int32 [1024], P(('wall', 'drops')), may hold values from 2 to 4
- patch_points: float32 [8192, 192], P('wall'), may hold values from -6 to 6
- patch_strength: float32 [8192, 192], P('wall'), may hold values from -1 to 1
- wall_near: int32 [1024, 8], P(('wall', 'drops')), may hold values from 0 to 8191
Outputs:
- drop_velocity: float32 [1024, 3, 544], P(('wall', 'drops'))
The draws below stay inside these ranges and needn't reach their ends.
Inputs may be any that keep to these rules, and one draw needn't show every extreme that they name: `near_drops`: each entry names a drop of the same drop group (same index along wall). Of the 32 entries of one device, at most 2 name drops of any one device of the group, and on every device some device of the group is named exactly 2 times. Entries at slots k >= near_count are ignored.
All inputs are finite; a program needn't handle non-finite values.
Results may differ from the reference program's by a relative error of at most 0.0003.
Values sent between devices are 32-bit elements; how exact they have to be, the bound alone decides.
No kernel may reach another device: no remote copies, remote signals or barrier semaphores. Data moves between devices by JAX's collectives and lax.ppermute only.
A program may use at most 128 MiB of HBM per device.

```python
import math
import jax
import jax.numpy as jnp
import numpy as np
from jax import lax

NC = 544
NU = 2112
PNODES = 64
K_NEAR = 4
K_WALL = 8
DROP_DEV = 8
GROUP_RANKS = 32
WALL_RANKS = 4
DROPS = 1024
PATCHES = 8192
CAP = 2


def draw_near_drops(key, part):
    entries = DROP_DEV * K_NEAR
    total_slots = GROUP_RANKS * CAP
    devices = WALL_RANKS * GROUP_RANKS
    keys = jax.random.split(key, devices)

    def one_device(device_key, device):
        first, second, third, fourth = jax.random.split(device_key, 4)
        group = device // GROUP_RANKS
        favored = jax.random.randint(first, (), 0, GROUP_RANKS)
        slot_owner = jnp.arange(total_slots, dtype=jnp.int32) // CAP
        score = jax.random.permutation(second, total_slots).astype(jnp.int32)
        score = jnp.where(slot_owner == favored, score - total_slots, score)
        order = jnp.argsort(score, stable=True)
        owners = slot_owner[order[:entries]]
        owners = owners[jax.random.permutation(third, entries)]
        local = jax.random.randint(fourth, (entries,), 0, DROP_DEV)
        picked = (group * GROUP_RANKS + owners) * DROP_DEV + local
        return picked.astype(jnp.int32).reshape(DROP_DEV, K_NEAR)
    every = jax.vmap(one_device)(keys, jnp.arange(devices, dtype=jnp.int32))
    return every.reshape(DROPS, K_NEAR)


def place_ends(array, own_key, least, high):
    longest = array.shape.index(max(array.shape))
    spots = []
    for shift in (0, 1):
        where = [jax.random.randint(jax.random.fold_in(own_key, axis), (), 0, length) for axis, length in enumerate(array.shape)]
        where[longest] = (where[longest] + shift) % array.shape[longest]
        spots.append(tuple(where))
    return array.at[spots[0]].set(least).at[spots[1]].set(high)


def steps_of(stream_key, extent, pieces, least, top_value):
    def one(dim, shards_of):
        steps = jax.random.uniform(jax.random.fold_in(jax.random.fold_in(stream_key, 6), dim), (shards_of,), jnp.float32, least / len(pieces), top_value / len(pieces))
        return jnp.repeat(jnp.exp(steps), extent[dim] // shards_of).reshape((-1,) + (1,) * (len(extent) - dim - 1))

    factor_of = one(*pieces[0])
    for cut in pieces[1:]:
        factor_of = factor_of * one(*cut)
    return factor_of


def rank_table(amount, skew):
    weights = [(1 << 20) // math.isqrt(grade ** skew) + 1 for grade in range(1, amount + 1)]
    spread = 1 + sum(weights) // (1 << 30)
    return np.cumsum(np.array([max(1, weight // spread) for weight in weights]))


def ranked(rng, shape, amount, lean):
    table = rank_table(amount, lean)
    lot = jax.random.randint(jax.random.fold_in(rng, 1), shape, 0, int(table[amount - 1]))
    grade = jnp.searchsorted(jnp.asarray(table, jnp.int32), lot, side="right")
    return jax.random.permutation(jax.random.fold_in(rng, 2), amount)[grade].astype(jnp.int32)


def normal_values(rng, extent, deviation, most, shards=(), held_as=jnp.bfloat16):
    values = deviation * jax.random.normal(rng, extent, jnp.float32)
    if shards:
        values = values * steps_of(rng, extent, shards, -0.22, 0.18)
    return jnp.clip(values, -most, most).astype(held_as)


def setup_inputs(seed: int = 0) -> dict:
    splits = jax.random.split(jax.random.key(seed), 10)
    return {
        "drop_points": normal_values(splits[0], (DROPS, 3, NC), 1.0, 6.0, ((0, 128),), jnp.float32),
        "drop_strength": normal_values(splits[1], (DROPS, 3, NC), (NU * K_NEAR // 16) ** -0.5, 0.25, ((0, 128),), jnp.float32),
        "upsample": normal_values(splits[2], (NC, NU), NC ** -0.5, 0.25, (), jnp.float32),
        "base_velocity": normal_values(splits[3], (DROPS, 3, NC), 1.0, 6.0, ((0, 128),), jnp.float32),
        "near_drops": draw_near_drops(jax.random.fold_in(splits[9], 71), 0),
        "near_count": place_ends(jax.random.randint(splits[5], (DROPS,), 2, K_NEAR + 1), jax.random.fold_in(splits[5], 1), 2, K_NEAR).astype(jnp.int32),
        "patch_points": normal_values(splits[6], (PATCHES, 3 * PNODES), 1.0, 6.0, ((0, 4),), jnp.float32),
        "patch_strength": normal_values(splits[7], (PATCHES, 3 * PNODES), (PNODES * K_WALL // 16) ** -0.5, 1.0, ((0, 4),), jnp.float32),
        "wall_near": place_ends(ranked(splits[8], (DROPS, K_WALL), PATCHES, 2), jax.random.fold_in(splits[8], 3), 0, PATCHES - 1).astype(jnp.int32),
    }


smoothing_square = 0.25

def stokes_sum(targets, sources, strength):
    delta = targets[:, :, None] - sources[:, None, :]
    dist = lax.optimization_barrier(jnp.sum(delta * delta, axis=0))
    inverse = lax.rsqrt(dist + smoothing_square)
    cubed = inverse * inverse * inverse
    along = lax.optimization_barrier(jnp.sum(delta * strength[:, None, :], axis=0))
    terms = ((dist + 2.0 * smoothing_square) * strength[:, None, :] + along * delta) * cubed
    return lax.optimization_barrier(jnp.sum(terms, axis=2))

def reference(drop_points, drop_strength, upsample, base_velocity, near_drops, near_count, patch_points, patch_strength, wall_near):

    def one_drop(index):
        targets = drop_points[index]
        listed = wall_near[index]
        wall_pts = patch_points[listed].reshape(K_WALL, 3, PNODES).transpose(1, 0, 2).reshape(3, K_WALL * PNODES)
        wall_str = patch_strength[listed].reshape(K_WALL, 3, PNODES).transpose(1, 0, 2).reshape(3, K_WALL * PNODES)
        total = base_velocity[index] + stokes_sum(targets, wall_pts, wall_str)
        for slot in range(K_NEAR):
            partner = near_drops[index, slot]
            coarse_pts = drop_points[partner]
            coarse_str = drop_strength[partner]
            fine_pts = jnp.dot(coarse_pts, upsample, preferred_element_type=jnp.float32, precision=lax.Precision.HIGHEST)
            fine_str = jnp.dot(coarse_str, upsample, preferred_element_type=jnp.float32, precision=lax.Precision.HIGHEST)
            sources = jnp.concatenate([fine_pts, coarse_pts], axis=1)
            strengths = jnp.concatenate([fine_str, -coarse_str], axis=1)
            term = stokes_sum(targets, sources, strengths)
            live = (slot < near_count[index]).astype(jnp.float32)
            total = total + live * term
        return total
    return lax.map(one_drop, jnp.arange(DROPS, dtype=jnp.int32))
```

```python
import functools

import jax
import jax.numpy as jnp
from jax import lax
from jax.experimental import pallas as pl
from jax.experimental.pallas import tpu as pltpu
from jax.sharding import PartitionSpec as P

smoothing_square = 0.25
f32 = jnp.float32
bf16 = jnp.bfloat16


def pieces(v, count):
    out = []
    for _ in range(count):
        p = lax.reduce_precision(v, 8, 7)
        out.append(p)
        v = v - p
    return out


def source_features(pts, strength):
    y = [pts[:, i] for i in range(3)]
    g = [strength[:, i] for i in range(3)]
    one = jnp.ones_like(y[0])
    zero = jnp.zeros_like(y[0])
    square = y[0] * y[0] + y[1] * y[1] + y[2] * y[2]
    rows = []
    for i in range(3):
        b = pieces(y[i], 3)
        rows += [b[0], b[1], b[2], b[0], b[1], b[2], b[0], b[1]]
    rows += pieces(square, 3) + [one, one, one, zero, zero]
    dist = jnp.stack(rows, axis=1).astype(bf16)
    along = y[0] * g[0] + y[1] * g[1] + y[2] * g[2]
    cols = list(g)
    cols += [y[b] * g[a] for b in range(3) for a in range(3)]
    cols += [(square + 2.0 * smoothing_square) * g[a] + along * y[a] for a in range(3)]
    cols += [zero]
    c3 = pieces(jnp.stack(cols, axis=1), 3)
    value = jnp.concatenate([c3[0], c3[1], c3[2], c3[0], c3[1]], axis=1).astype(bf16)
    return dist, value


def target_features(targets):
    x = [targets[:, i] for i in range(3)]
    one = jnp.ones_like(x[0])
    zero = jnp.zeros_like(x[0])
    square = x[0] * x[0] + x[1] * x[1] + x[2] * x[2]
    rows = []
    for i in range(3):
        a = pieces(-2.0 * x[i], 3)
        rows += [a[0], a[0], a[0], a[1], a[1], a[1], a[2], a[2]]
    rows += [one, one, one] + pieces(square + smoothing_square, 3) + [zero, zero]
    return jnp.stack(rows, axis=1).astype(bf16)


def pair_kernel(count_ref, x_ref, t_ref, b_ref, d_ref, v_ref, o_ref, acc_ref):
    slot = pl.program_id(1)

    @pl.when(slot == 0)
    def _():
        acc_ref[...] = jnp.zeros_like(acc_ref)

    @pl.when(slot < count_ref[pl.program_id(0)])
    def _():
        dist = lax.dot_general(
            d_ref[0], x_ref[0], (((0,), (0,)), ((), ())), preferred_element_type=f32
        )
        w = lax.rsqrt(dist)
        w3 = w * w * w
        hi = w3.astype(bf16)
        lo = (w3 - hi.astype(f32)).astype(bf16)
        acc_ref[:48] += jnp.dot(v_ref[0, :48], hi, preferred_element_type=f32)
        acc_ref[48:] += jnp.dot(v_ref[0, 48:], lo, preferred_element_type=f32)

    @pl.when(slot == pl.num_programs(1) - 1)
    def _():
        q = acc_ref[0:16] + acc_ref[16:32] + acc_ref[32:48] + (acc_ref[48:64] + acc_ref[64:80])
        x = [t_ref[0, i : i + 1] for i in range(3)]
        square = x[0] * x[0] + x[1] * x[1] + x[2] * x[2]
        gs = [q[a : a + 1] for a in range(3)]
        h = [[q[3 + 3 * b + a : 4 + 3 * b + a] for a in range(3)] for b in range(3)]
        m = [q[12 + a : 13 + a] for a in range(3)]
        lean = x[0] * gs[0] + x[1] * gs[1] + x[2] * gs[2] - (h[0][0] + h[1][1] + h[2][2])
        for a in range(3):
            u = m[a] + square * gs[a] + x[a] * lean
            for b in range(3):
                u = u - x[b] * (2.0 * h[b][a] + h[a][b])
            o_ref[0, a : a + 1] = b_ref[0, a : a + 1] + u


def pair_sums(counts, feats, targets, base, dist, value, slots, name):
    owned, _, nodes = targets.shape
    width = dist.shape[2]

    def src(i, k, c):
        return (i * slots + jnp.minimum(k, c[i] - 1), 0, 0)

    def drop(i, k, c):
        return (i, 0, 0)

    return pl.pallas_call(
        pair_kernel,
        grid_spec=pltpu.PrefetchScalarGridSpec(
            num_scalar_prefetch=1,
            grid=(owned, slots),
            in_specs=[
                pl.BlockSpec((1, 32, nodes), drop),
                pl.BlockSpec((1, 3, nodes), drop),
                pl.BlockSpec((1, 3, nodes), drop),
                pl.BlockSpec((1, 32, width), src),
                pl.BlockSpec((1, 80, width), src),
            ],
            out_specs=pl.BlockSpec((1, 3, nodes), drop),
            scratch_shapes=[pltpu.VMEM((80, nodes), f32)],
        ),
        out_shape=jax.ShapeDtypeStruct(targets.shape, f32),
        name=name,
    )(counts, feats, targets, base, dist, value)


def per_device(
    drop_points,
    drop_strength,
    upsample,
    base_velocity,
    near_drops,
    near_count,
    patch_points,
    patch_strength,
    wall_near,
):
    ranks = lax.axis_size("drops")
    walls = lax.axis_size("wall")
    owned, _, coarse = drop_points.shape
    fine = upsample.shape[1]
    slots = near_drops.shape[1]
    entries = owned * slots
    depth = max(2, (entries + ranks - 1) // ranks)

    partner = near_drops.reshape(entries)
    owner = partner // owned % ranks
    local = partner % owned
    member = (owner[:, None] == jnp.arange(ranks, dtype=jnp.int32)[None, :]).astype(jnp.int32)
    position = jnp.sum((jnp.cumsum(member, axis=0) - 1) * member, axis=1)
    slot_hit = member[:, :, None] * (
        position[:, None, None] == jnp.arange(depth, dtype=jnp.int32)[None, None, :]
    ).astype(jnp.int32)
    requests = jnp.sum(slot_hit * local[:, None, None], axis=0)
    incoming = lax.all_to_all(requests, "drops", split_axis=0, concat_axis=0, tiled=True)

    held = patch_points.shape[0]
    listed = wall_near.shape[1]
    wanted = wall_near.reshape(owned * listed)
    asked = lax.all_to_all(
        jnp.broadcast_to(wanted[None], (walls, owned * listed)),
        "wall", split_axis=0, concat_axis=0, tiled=True,
    )

    both = jnp.concatenate([drop_points, drop_strength], axis=1)
    send = jnp.take(both, incoming.reshape(ranks * depth), axis=0)
    got = lax.all_to_all(
        send.reshape(ranks, depth, 6, coarse), "drops", split_axis=0, concat_axis=0, tiled=True
    )

    index = jnp.clip(asked - lax.axis_index("wall") * held, 0, held - 1).reshape(-1)
    rows = jnp.concatenate(
        [jnp.take(patch_points, index, axis=0), jnp.take(patch_strength, index, axis=0)], axis=1
    )
    width = rows.shape[1]
    back = lax.all_to_all(
        rows.reshape(walls, owned * listed, width), "wall", split_axis=0, concat_axis=0, tiled=True
    )
    home = wanted // held
    mine = jnp.zeros((owned * listed, width), f32)
    for r in range(walls):
        mine = jnp.where((home == r)[:, None], back[r], mine)
    patch = width // 6
    mine = mine.reshape(owned, listed, 6, patch).transpose(0, 2, 1, 3).reshape(owned, 6, -1)

    feats = target_features(drop_points)
    wall_dist, wall_value = source_features(mine[:, :3], mine[:, 3:])
    total = pair_sums(
        jnp.ones((owned,), jnp.int32), feats, drop_points, base_velocity,
        wall_dist, wall_value, 1, "wall_pairs",
    )

    source = jnp.take(got.reshape(ranks * depth, 6, coarse), owner * depth + position, axis=0)
    finer = jnp.einsum("ecn,nu->ecu", source, upsample, precision=lax.Precision.HIGHEST)
    pad = -(fine + coarse) % 128
    sign = jnp.array([1, 1, 1, -1, -1, -1], f32)[None, :, None]
    joined = jnp.concatenate(
        [finer, source * sign, jnp.zeros((entries, 6, pad), f32)], axis=2
    )
    near_dist, near_value = source_features(joined[:, :3], joined[:, 3:])
    return pair_sums(
        near_count, feats, drop_points, total, near_dist, near_value, slots, "near_pairs"
    )


def solution(mesh):
    return jax.shard_map(
        per_device,
        mesh=mesh,
        in_specs=(
            P(("wall", "drops"), None, None),
            P(("wall", "drops"), None, None),
            P(),
            P(("wall", "drops"), None, None),
            P(("wall", "drops"), None),
            P(("wall", "drops")),
            P("wall", None),
            P("wall", None),
            P(("wall", "drops"), None),
        ),
        out_specs=P(("wall", "drops"), None, None),
        check_vma=False,
    )
```

```python
import functools

import jax
import jax.numpy as jnp
from jax import lax
from jax.experimental import pallas as pl
from jax.experimental.pallas import tpu as pltpu
from jax.sharding import PartitionSpec as P

smoothing_square = 0.25
f32 = jnp.float32
bf16 = jnp.bfloat16


def nn(a, b):
    return jnp.dot(a, b, preferred_element_type=f32)


def split(v, count):
    out = []
    for left in reversed(range(count)):
        p = v.astype(bf16)
        out.append(p)
        if left:
            v = v - p.astype(f32)
    return out


def write_rows(q_ref, where, first, y, g):
    n = y[0].shape[0]
    at = slice(first, first + n)
    square = y[0] * y[0] + y[1] * y[1] + y[2] * y[2]
    along = y[0] * g[0] + y[1] * g[1] + y[2] * g[2]
    rows = list(g)
    rows += [y[b] * g[a] for b in range(3) for a in range(3)]
    rows += [(square + 2.0 * smoothing_square) * g[a] + along * y[a] for a in range(3)]
    rows += [jnp.zeros_like(square)]
    for _ in range(3):
        rows += y + [square]
    rows += [jnp.ones_like(square)] * 4
    for r, row in enumerate(rows):
        q_ref[at, r, where] = row


def source_rows(q):
    c = split(q[:16], 3)
    b = split(q[16:], 3)
    row = lax.broadcasted_iota(jnp.int32, b[0].shape, 0)
    hi, mid, lo = [p.astype(f32) for p in b]
    first = jnp.where(row < 4, hi, jnp.where(row < 8, mid, jnp.where(row < 12, lo, hi)))
    second = jnp.where((row >= 4) & (row < 8), mid, hi)
    dist = jnp.concatenate([first.astype(bf16), second.astype(bf16)], axis=0)
    return dist, jnp.concatenate(c, axis=0), jnp.concatenate(c[:2], axis=0)


def target_rows(x):
    square = x[0] * x[0] + x[1] * x[1] + x[2] * x[2] + smoothing_square
    one = jnp.ones_like(square)
    zero = jnp.zeros_like(square)
    a = [split(-2.0 * v, 3) for v in x]
    a = [[p.astype(f32) for p in v] for v in a]
    s = [p.astype(f32) for p in split(square, 3)]
    top = [a[0][0], a[1][0], a[2][0], one]
    rows = top * 3 + s + [zero]
    rows += [a[0][1], a[1][1], a[2][1], zero] * 2
    rows += [a[0][2], a[1][2], a[2][2], zero] + [zero] * 4
    return jnp.concatenate(rows, axis=0).astype(bf16)


def accumulate(acc_ref, xf, q):
    dist_rows, three, two = source_rows(q)
    dist = lax.dot_general(dist_rows, xf, (((0,), (0,)), ((), ())), preferred_element_type=f32)
    w = lax.rsqrt(dist)
    w3 = w * w * w
    hi = w3.astype(bf16)
    lo = (w3 - hi.astype(f32)).astype(bf16)
    acc_ref[:48] += nn(three, hi)
    acc_ref[48:] += nn(two, lo)


def pair_kernel(
    count_ref, pick_ref, got_ref, up_ref, wall_ref, t_ref, b_ref, o_ref,
    cbuf, q_ref, p_ref, acc_ref, xf_ref,
):
    drop = pl.program_id(0)
    slot = pl.program_id(1)
    slots = pl.num_programs(1)
    entries = q_ref.shape[0]
    coarse = got_ref.shape[2]
    fine = up_ref.shape[1]

    @pl.when((drop == 0) & (slot == 0))
    def _():
        for e in range(entries):
            cbuf[:, e, :] = got_ref[pick_ref[e]]
        source = [cbuf[c] for c in range(6)]
        parts = [split(v, 2) for v in source]
        high = jnp.concatenate([p[0] for p in parts], axis=0)
        low = jnp.concatenate([p[1] for p in parts], axis=0)
        step = 384
        for u0 in range(0, fine, step):
            u1 = min(fine, u0 + step)
            up = split(up_ref[:, u0:u1], 2)
            f = nn(high, up[0]) + (nn(low, up[0]) + nn(high, up[1]))
            f = [f[c * entries : (c + 1) * entries] for c in range(6)]
            write_rows(q_ref, slice(u0, u1), 0, f[:3], f[3:])
        tail = q_ref.shape[2] - fine - coarse
        full = [jnp.concatenate([v, jnp.zeros((entries, tail), f32)], axis=1) for v in source]
        write_rows(q_ref, slice(fine, q_ref.shape[2]), 0, full[:3], [-v for v in full[3:]])
        w = [wall_ref[c] for c in range(6)]
        write_rows(p_ref, slice(0, p_ref.shape[2]), 0, w[:3], w[3:])

    @pl.when(slot == 0)
    def _():
        x = [t_ref[0, i : i + 1] for i in range(3)]
        xf_ref[...] = target_rows(x)
        acc_ref[...] = jnp.zeros_like(acc_ref)
        accumulate(acc_ref, xf_ref[...], p_ref[drop])

    @pl.when(slot < count_ref[drop])
    def _():
        accumulate(acc_ref, xf_ref[...], q_ref[drop * slots + slot])

    @pl.when(slot == slots - 1)
    def _():
        q = acc_ref[0:16] + acc_ref[16:32] + acc_ref[32:48] + (acc_ref[48:64] + acc_ref[64:80])
        x = [t_ref[0, i : i + 1] for i in range(3)]
        square = x[0] * x[0] + x[1] * x[1] + x[2] * x[2]
        gs = [q[a : a + 1] for a in range(3)]
        h = [[q[3 + 3 * b + a : 4 + 3 * b + a] for a in range(3)] for b in range(3)]
        m = [q[12 + a : 13 + a] for a in range(3)]
        lean = x[0] * gs[0] + x[1] * gs[1] + x[2] * gs[2] - (h[0][0] + h[1][1] + h[2][2])
        for a in range(3):
            u = m[a] + square * gs[a] + x[a] * lean
            for b in range(3):
                u = u - x[b] * (2.0 * h[b][a] + h[a][b])
            o_ref[0, a : a + 1] = b_ref[0, a : a + 1] + u


def pair_sums(counts, pick, got, upsample, wall, targets, base):
    owned, _, nodes = targets.shape
    entries = pick.shape[0]
    slots = entries // owned
    fine = upsample.shape[1]
    width = -(-(fine + nodes) // 128) * 128

    def whole(a):
        return pl.BlockSpec(a.shape, lambda i, k, c, p: (0,) * a.ndim, pipeline_mode=pl.Buffered(1))

    per_drop = pl.BlockSpec((1, 3, nodes), lambda i, k, c, p: (i, 0, 0))
    return pl.pallas_call(
        pair_kernel,
        grid_spec=pltpu.PrefetchScalarGridSpec(
            num_scalar_prefetch=2,
            grid=(owned, slots),
            in_specs=[whole(got), whole(upsample), whole(wall), per_drop, per_drop],
            out_specs=per_drop,
            scratch_shapes=[
                pltpu.VMEM((6, entries, nodes), f32),
                pltpu.VMEM((entries, 32, width), f32),
                pltpu.VMEM((owned, 32, wall.shape[2]), f32),
                pltpu.VMEM((80, nodes), f32),
                pltpu.VMEM((32, nodes), bf16),
            ],
        ),
        out_shape=jax.ShapeDtypeStruct(targets.shape, f32),
        name="pairs",
    )(counts, pick, got, upsample, wall, targets, base)


def per_device(
    drop_points,
    drop_strength,
    upsample,
    base_velocity,
    near_drops,
    near_count,
    patch_points,
    patch_strength,
    wall_near,
):
    ranks = lax.axis_size("drops")
    walls = lax.axis_size("wall")
    owned, _, coarse = drop_points.shape
    fine = upsample.shape[1]
    slots = near_drops.shape[1]
    entries = owned * slots
    depth = max(2, (entries + ranks - 1) // ranks)

    partner = near_drops.reshape(entries)
    owner = partner // owned % ranks
    local = partner % owned
    member = (owner[:, None] == jnp.arange(ranks, dtype=jnp.int32)[None, :]).astype(jnp.int32)
    position = jnp.sum((jnp.cumsum(member, axis=0) - 1) * member, axis=1)
    slot_hit = member[:, :, None] * (
        position[:, None, None] == jnp.arange(depth, dtype=jnp.int32)[None, None, :]
    ).astype(jnp.int32)
    requests = jnp.sum(slot_hit * local[:, None, None], axis=0)
    incoming = lax.all_to_all(requests, "drops", split_axis=0, concat_axis=0, tiled=True)

    held = patch_points.shape[0]
    listed = wall_near.shape[1]
    wanted = wall_near.reshape(owned * listed)
    asked = lax.all_to_all(
        jnp.broadcast_to(wanted[None], (walls, owned * listed)),
        "wall", split_axis=0, concat_axis=0, tiled=True,
    )

    both = jnp.concatenate([drop_points, drop_strength], axis=1)
    send = jnp.take(both, incoming.reshape(ranks * depth), axis=0)
    got = lax.all_to_all(
        send.reshape(ranks, depth, 6, coarse), "drops", split_axis=0, concat_axis=0, tiled=True
    )

    index = jnp.clip(asked - lax.axis_index("wall") * held, 0, held - 1).reshape(-1)
    rows = jnp.concatenate(
        [jnp.take(patch_points, index, axis=0), jnp.take(patch_strength, index, axis=0)], axis=1
    )
    width = rows.shape[1]
    back = lax.all_to_all(
        rows.reshape(walls, owned * listed, width), "wall", split_axis=0, concat_axis=0, tiled=True
    )
    home = wanted // held
    mine = jnp.zeros((owned * listed, width), f32)
    for r in range(walls):
        mine = jnp.where((home == r)[:, None], back[r], mine)
    patch = width // 6
    mine = mine.reshape(owned, listed, 6, patch).transpose(2, 0, 1, 3).reshape(6, owned, -1)
    return pair_sums(
        near_count,
        owner * depth + position,
        got.reshape(ranks * depth, 6, coarse),
        upsample,
        mine,
        drop_points,
        base_velocity,
    )


def solution(mesh):
    return jax.shard_map(
        per_device,
        mesh=mesh,
        in_specs=(
            P(("wall", "drops"), None, None),
            P(("wall", "drops"), None, None),
            P(),
            P(("wall", "drops"), None, None),
            P(("wall", "drops"), None),
            P(("wall", "drops")),
            P("wall", None),
            P("wall", None),
            P(("wall", "drops"), None),
        ),
        out_specs=P(("wall", "drops"), None, None),
        check_vma=False,
    )
```

```python
import jax
import jax.numpy as jnp
from jax import lax
from jax.experimental import pallas as pl
from jax.experimental.pallas import tpu as pltpu
from jax.sharding import PartitionSpec as P

smoothing_square = 0.25
f32 = jnp.float32
bf16 = jnp.bfloat16


def nn(a, b):
    return jnp.dot(a, b, preferred_element_type=f32)


def split(v, count):
    out = []
    for left in reversed(range(count)):
        p = v.astype(bf16)
        out.append(p)
        if left:
            v = v - p.astype(f32)
    return out


def write_rows(q_ref, where, first, y, g):
    n = y[0].shape[0]
    at = slice(first, first + n)
    square = y[0] * y[0] + y[1] * y[1] + y[2] * y[2]
    along = y[0] * g[0] + y[1] * g[1] + y[2] * g[2]
    rows = list(g)
    rows += [y[b] * g[a] for b in range(3) for a in range(3)]
    rows += [(square + 2.0 * smoothing_square) * g[a] + along * y[a] for a in range(3)]
    rows += [jnp.zeros_like(square)]
    for _ in range(3):
        rows += y + [square]
    rows += [jnp.ones_like(square)] * 4
    for r, row in enumerate(rows):
        q_ref[at, r, where] = row


def source_rows(q):
    c = split(q[:16], 3)
    b = split(q[16:], 3)
    row = lax.broadcasted_iota(jnp.int32, b[0].shape, 0)
    hi, mid, lo = [p.astype(f32) for p in b]
    first = jnp.where(row < 4, hi, jnp.where(row < 8, mid, jnp.where(row < 12, lo, hi)))
    second = jnp.where((row >= 4) & (row < 8), mid, hi)
    dist = jnp.concatenate([first.astype(bf16), second.astype(bf16)], axis=0)
    return dist, jnp.concatenate(c, axis=0), jnp.concatenate(c[:2], axis=0)


def target_rows(x):
    square = x[0] * x[0] + x[1] * x[1] + x[2] * x[2] + smoothing_square
    one = jnp.ones_like(square)
    zero = jnp.zeros_like(square)
    a = [split(-2.0 * v, 3) for v in x]
    a = [[p.astype(f32) for p in v] for v in a]
    s = [p.astype(f32) for p in split(square, 3)]
    top = [a[0][0], a[1][0], a[2][0], one]
    rows = top * 3 + s + [zero]
    rows += [a[0][1], a[1][1], a[2][1], zero] * 2
    rows += [a[0][2], a[1][2], a[2][2], zero] + [zero] * 4
    return jnp.concatenate(rows, axis=0).astype(bf16)


def accumulate(acc_ref, xf, q):
    dist_rows, three, two = source_rows(q)
    dist = lax.dot_general(dist_rows, xf, (((0,), (0,)), ((), ())), preferred_element_type=f32)
    w = lax.rsqrt(dist)
    w3 = w * w * w
    hi = w3.astype(bf16)
    lo = (w3 - hi.astype(f32)).astype(bf16)
    acc_ref[:48] += nn(three, hi)
    acc_ref[48:] += nn(two, lo)


def finish(acc_ref, t_ref, b_ref, o_ref, drop):
    q = acc_ref[0:16] + acc_ref[16:32] + acc_ref[32:48] + (acc_ref[48:64] + acc_ref[64:80])
    at = pl.ds(drop, 1)
    x = [t_ref[i, at] for i in range(3)]
    square = x[0] * x[0] + x[1] * x[1] + x[2] * x[2]
    gs = [q[a : a + 1] for a in range(3)]
    h = [[q[3 + 3 * b + a : 4 + 3 * b + a] for a in range(3)] for b in range(3)]
    m = [q[12 + a : 13 + a] for a in range(3)]
    lean = x[0] * gs[0] + x[1] * gs[1] + x[2] * gs[2] - (h[0][0] + h[1][1] + h[2][2])
    for a in range(3):
        u = m[a] + square * gs[a] + x[a] * lean
        for b in range(3):
            u = u - x[b] * (2.0 * h[b][a] + h[a][b])
        o_ref[a, at] = b_ref[a, at] + u


def wall_kernel(wall_ref, t_ref, b_ref, o_ref, p_ref, acc_ref):
    drop = pl.program_id(0)

    @pl.when(drop == 0)
    def _():
        w = [wall_ref[c] for c in range(6)]
        write_rows(p_ref, slice(0, p_ref.shape[2]), 0, w[:3], w[3:])

    acc_ref[...] = jnp.zeros_like(acc_ref)
    xf = target_rows([t_ref[i, pl.ds(drop, 1)] for i in range(3)])
    accumulate(acc_ref, xf, p_ref[drop])
    finish(acc_ref, t_ref, b_ref, o_ref, drop)


def near_kernel(
    count_ref, pick_ref, got_ref, up_ref, t_ref, b_ref, o_ref,
    cbuf, q_ref, acc_ref, xf_ref,
):
    drop = pl.program_id(0)
    slot = pl.program_id(1)
    slots = pl.num_programs(1)
    entries = q_ref.shape[0]
    depth = got_ref.shape[2]
    coarse = got_ref.shape[3]
    fine = up_ref.shape[1]

    @pl.when((drop == 0) & (slot == 0))
    def _():
        for e in range(entries):
            both = got_ref[pick_ref[e] // depth]
            place = pick_ref[e] % depth
            row = both[:, 0]
            for p in range(1, depth):
                row = jnp.where(place == p, both[:, p], row)
            cbuf[:, e, :] = row
        source = [cbuf[c] for c in range(6)]
        parts = [split(v, 2) for v in source]
        high = jnp.concatenate([p[0] for p in parts], axis=0)
        low = jnp.concatenate([p[1] for p in parts], axis=0)
        step = 384
        for u0 in range(0, fine, step):
            u1 = min(fine, u0 + step)
            up = split(up_ref[:, u0:u1], 2)
            f = nn(high, up[0]) + (nn(low, up[0]) + nn(high, up[1]))
            f = [f[c * entries : (c + 1) * entries] for c in range(6)]
            write_rows(q_ref, slice(u0, u1), 0, f[:3], f[3:])
        tail = q_ref.shape[2] - fine - coarse
        full = [jnp.concatenate([v, jnp.zeros((entries, tail), f32)], axis=1) for v in source]
        write_rows(q_ref, slice(fine, q_ref.shape[2]), 0, full[:3], [-v for v in full[3:]])

    @pl.when(slot == 0)
    def _():
        xf_ref[...] = target_rows([t_ref[i, pl.ds(drop, 1)] for i in range(3)])
        acc_ref[...] = jnp.zeros_like(acc_ref)

    @pl.when(slot < count_ref[drop])
    def _():
        accumulate(acc_ref, xf_ref[...], q_ref[drop * slots + slot])

    @pl.when(slot == slots - 1)
    def _():
        finish(acc_ref, t_ref, b_ref, o_ref, drop)


def whole(a):
    zeros = (0,) * len(a.shape)
    return pl.BlockSpec(a.shape, lambda *_: zeros, pipeline_mode=pl.Buffered(1))


def wall_sums(wall, targets, base):
    _, owned, nodes = targets.shape
    return pl.pallas_call(
        wall_kernel,
        grid=(owned,),
        in_specs=[whole(wall), whole(targets), whole(base)],
        out_specs=whole(targets),
        scratch_shapes=[
            pltpu.VMEM((owned, 32, wall.shape[2]), f32),
            pltpu.VMEM((80, nodes), f32),
        ],
        out_shape=jax.ShapeDtypeStruct(targets.shape, f32),
        name="wall_pairs",
    )(wall, targets, base)


def near_sums(counts, pick, got, upsample, targets, base):
    _, owned, nodes = targets.shape
    entries = pick.shape[0]
    slots = entries // owned
    width = -(-(upsample.shape[1] + nodes) // 128) * 128
    return pl.pallas_call(
        near_kernel,
        grid_spec=pltpu.PrefetchScalarGridSpec(
            num_scalar_prefetch=2,
            grid=(owned, slots),
            in_specs=[whole(got), whole(upsample), whole(targets), whole(base)],
            out_specs=whole(targets),
            scratch_shapes=[
                pltpu.VMEM((6, entries, nodes), f32),
                pltpu.VMEM((entries, 32, width), f32),
                pltpu.VMEM((80, nodes), f32),
                pltpu.VMEM((32, nodes), bf16),
            ],
        ),
        out_shape=jax.ShapeDtypeStruct(targets.shape, f32),
        name="near_pairs",
    )(counts, pick, got, upsample, targets, base)


def per_device(
    drop_points,
    drop_strength,
    upsample,
    base_velocity,
    near_drops,
    near_count,
    patch_points,
    patch_strength,
    wall_near,
):
    ranks = lax.axis_size("drops")
    walls = lax.axis_size("wall")
    owned, _, coarse = drop_points.shape
    slots = near_drops.shape[1]
    entries = owned * slots
    depth = max(2, (entries + ranks - 1) // ranks)
    here = lax.axis_index("wall")

    held = patch_points.shape[0]
    listed = wall_near.shape[1]
    wanted = wall_near.reshape(owned * listed)
    asked = [wanted] + [
        lax.ppermute(wanted, "wall", [(w, (w + r) % walls) for w in range(walls)])
        for r in range(1, walls)
    ]

    partner = near_drops.reshape(entries)
    owner = partner // owned % ranks
    local = partner % owned
    member = (owner[:, None] == jnp.arange(ranks, dtype=jnp.int32)[None, :]).astype(jnp.int32)
    position = jnp.sum((jnp.cumsum(member, axis=0) - 1) * member, axis=1)
    slot_hit = member[:, :, None] * (
        position[:, None, None] == jnp.arange(depth, dtype=jnp.int32)[None, None, :]
    ).astype(jnp.int32)
    requests = jnp.sum(slot_hit * local[:, None, None], axis=0)
    incoming = lax.all_to_all(requests, "drops", split_axis=0, concat_axis=0, tiled=True)

    index = jnp.clip(jnp.concatenate(asked) - here * held, 0, held - 1)
    rows = jnp.concatenate(
        [jnp.take(patch_points, index, axis=0), jnp.take(patch_strength, index, axis=0)], axis=1
    )
    rows = rows.reshape(walls, owned * listed, -1)
    home = wanted // held
    mine = rows[0]
    for r in range(1, walls):
        back = lax.ppermute(rows[r], "wall", [(w, (w - r) % walls) for w in range(walls)])
        mine = jnp.where((home == (here + r) % walls)[:, None], back, mine)
    patch = rows.shape[2] // 6
    mine = mine.reshape(owned, listed, 6, patch).transpose(2, 0, 1, 3).reshape(6, owned, -1)

    both = jnp.concatenate([drop_points, drop_strength], axis=1)
    send = jnp.take(both, incoming.reshape(ranks * depth), axis=0)
    send = send.reshape(ranks, depth, 6, coarse).transpose(0, 2, 1, 3)
    got = lax.all_to_all(send, "drops", split_axis=0, concat_axis=0, tiled=True)

    targets = drop_points.transpose(1, 0, 2)
    total = wall_sums(mine, targets, base_velocity.transpose(1, 0, 2))
    total = near_sums(near_count, owner * depth + position, got, upsample, targets, total)
    return total.transpose(1, 0, 2)


def solution(mesh):
    return jax.shard_map(
        per_device,
        mesh=mesh,
        in_specs=(
            P(("wall", "drops"), None, None),
            P(("wall", "drops"), None, None),
            P(),
            P(("wall", "drops"), None, None),
            P(("wall", "drops"), None),
            P(("wall", "drops")),
            P("wall", None),
            P("wall", None),
            P(("wall", "drops"), None),
        ),
        out_specs=P(("wall", "drops"), None, None),
        check_vma=False,
    )
```

```python
import jax
import jax.numpy as jnp
from jax import lax
from jax.experimental import pallas as pl
from jax.experimental.pallas import tpu as pltpu
from jax.sharding import PartitionSpec as P


smoothing_square = 0.25
f32 = jnp.float32
bf16 = jnp.bfloat16


def nn(a, b):
    return jnp.dot(a, b, preferred_element_type=f32)


def split(v, count):
    out = []
    for left in reversed(range(count)):
        p = v.astype(bf16)
        out.append(p)
        if left:
            v = v - p.astype(f32)
    return out


def source_rows(row):
    y = [row(c) for c in range(3)]
    g = [row(3 + c) for c in range(3)]
    width = y[0].shape[1]
    y = [jnp.broadcast_to(v, (8, width)) for v in y]
    g = [jnp.broadcast_to(v, (8, width)) for v in g]
    at = lax.broadcasted_iota(jnp.int32, (8, width), 0)

    def lay(*values):
        out = values[-1]
        for r in range(len(values) - 2, -1, -1):
            if values[r] is not values[r + 1]:
                out = jnp.where(at <= r, values[r], out)
        return out

    one = jnp.ones((8, width), f32)
    zero = jnp.zeros((8, width), f32)
    square = y[0] * y[0] + y[1] * y[1] + y[2] * y[2]
    along = y[0] * g[0] + y[1] * g[1] + y[2] * g[2]
    grown = square + 2.0 * smoothing_square
    top = lay(g[0], g[1], g[2], g[0], g[1], g[2], g[0], g[1]) * lay(
        one, one, one, y[0], y[0], y[0], y[1], y[1]
    )
    low = lay(g[2], g[0], g[1], g[2], g[0], g[1], g[2], g[2]) * lay(
        y[1], y[2], y[2], y[2], grown, grown, grown, zero
    ) + along * lay(zero, zero, zero, zero, y[0], y[1], y[2], zero)
    c = split(jnp.concatenate([top, low], axis=0), 3)
    b = [p.astype(f32) for p in split(lay(y[0], y[1], y[2], square, y[0], y[1], y[2], square), 3)]
    first = jnp.where(at < 4, b[0], b[1])
    second = jnp.where(at < 4, b[2], one)
    dist = jnp.concatenate([first, second, first, b[0]], axis=0).astype(bf16)
    return dist, jnp.concatenate(c, axis=0), jnp.concatenate(c[:2], axis=0)


def target_rows(x):
    square = x[0] * x[0] + x[1] * x[1] + x[2] * x[2] + smoothing_square
    one = jnp.ones_like(square)
    zero = jnp.zeros_like(square)
    a = [split(-2.0 * v, 3) for v in x]
    a = [[p.astype(f32) for p in v] for v in a]
    s = [p.astype(f32) for p in split(square, 3)]
    top = [a[0][0], a[1][0], a[2][0], one]
    rows = top * 3 + s + [zero]
    rows += [a[0][1], a[1][1], a[2][1], zero] * 2
    rows += [a[0][2], a[1][2], a[2][2], zero] + [zero] * 4
    return jnp.concatenate(rows, axis=0).astype(bf16)


def accumulate(acc_ref, xf, row):
    dist_rows, three, two = source_rows(row)
    dist = lax.dot_general(dist_rows, xf, (((0,), (0,)), ((), ())), preferred_element_type=f32)
    w = lax.rsqrt(dist)
    w3 = w * w * w
    hi = w3.astype(bf16)
    lo = (w3 - hi.astype(f32)).astype(bf16)
    acc_ref[:48] += nn(three, hi)
    acc_ref[48:] += nn(two, lo)


def finish(acc_ref, t_ref, b_ref, o_ref, drop):
    q = acc_ref[0:16] + acc_ref[16:32] + acc_ref[32:48] + (acc_ref[48:64] + acc_ref[64:80])
    at = pl.ds(drop, 1)
    x = [t_ref[i, at] for i in range(3)]
    square = x[0] * x[0] + x[1] * x[1] + x[2] * x[2]
    gs = [q[a : a + 1] for a in range(3)]
    h = [[q[3 + 3 * b + a : 4 + 3 * b + a] for a in range(3)] for b in range(3)]
    m = [q[12 + a : 13 + a] for a in range(3)]
    lean = x[0] * gs[0] + x[1] * gs[1] + x[2] * gs[2] - (h[0][0] + h[1][1] + h[2][2])
    for a in range(3):
        u = m[a] + square * gs[a] + x[a] * lean
        for b in range(3):
            u = u - x[b] * (2.0 * h[b][a] + h[a][b])
        o_ref[a, at] = b_ref[a, at] + u


def wall_kernel(wall_ref, t_ref, b_ref, o_ref, acc_ref):
    drop = pl.program_id(0)
    acc_ref[...] = jnp.zeros_like(acc_ref)
    xf = target_rows([t_ref[i, pl.ds(drop, 1)] for i in range(3)])
    accumulate(acc_ref, xf, lambda c: wall_ref[drop, c : c + 1])
    finish(acc_ref, t_ref, b_ref, o_ref, drop)


def near_kernel(
    count_ref, pick_ref, got_ref, up_ref, t_ref, b_ref, o_ref,
    cbuf, f_ref, acc_ref, xf_ref,
):
    drop = pl.program_id(0)
    slot = pl.program_id(1)
    slots = pl.num_programs(1)
    entries = f_ref.shape[0]
    depth = got_ref.shape[2]
    coarse = got_ref.shape[3]
    fine = up_ref.shape[1]

    @pl.when((drop == 0) & (slot == 0))
    def _():
        pad = jnp.zeros((2, coarse), f32)
        for e in range(entries):
            both = got_ref[pick_ref[e] // depth]
            place = pick_ref[e] % depth
            row = both[:, 0]
            for p in range(1, depth):
                row = jnp.where(place == p, both[:, p], row)
            cbuf[e] = jnp.concatenate([row, pad], axis=0)
        source = cbuf[...]
        high, low = split(source.reshape(entries * 8, coarse), 2)
        step = 384
        for u0 in range(0, fine, step):
            u1 = min(fine, u0 + step)
            up = split(up_ref[:, u0:u1], 2)
            f = nn(high, up[0]) + (nn(low, up[0]) + nn(high, up[1]))
            f_ref[:, :, u0:u1] = f.reshape(entries, 8, u1 - u0)
        tail = f_ref.shape[2] - fine - coarse
        at = lax.broadcasted_iota(jnp.int32, source.shape, 1)
        source = jnp.where(at < 3, source, -source)
        f_ref[:, :, fine:] = jnp.concatenate(
            [source, jnp.zeros((entries, 8, tail), f32)], axis=2
        )

    @pl.when(slot == 0)
    def _():
        xf_ref[...] = target_rows([t_ref[i, pl.ds(drop, 1)] for i in range(3)])
        acc_ref[...] = jnp.zeros_like(acc_ref)

    @pl.when(slot < count_ref[drop])
    def _():
        accumulate(acc_ref, xf_ref[...], lambda c: f_ref[drop * slots + slot, c : c + 1])

    @pl.when(slot == slots - 1)
    def _():
        finish(acc_ref, t_ref, b_ref, o_ref, drop)


def whole(a):
    zeros = (0,) * len(a.shape)
    return pl.BlockSpec(a.shape, lambda *_: zeros, pipeline_mode=pl.Buffered(1))


def wall_sums(wall, targets, base):
    _, owned, nodes = targets.shape
    return pl.pallas_call(
        wall_kernel,
        grid=(owned,),
        in_specs=[whole(wall), whole(targets), whole(base)],
        out_specs=whole(targets),
        scratch_shapes=[
            pltpu.VMEM((80, nodes), f32),
        ],
        out_shape=jax.ShapeDtypeStruct(targets.shape, f32),
        name="wall_pairs",
    )(wall, targets, base)


def near_sums(counts, pick, got, upsample, targets, base):
    _, owned, nodes = targets.shape
    entries = pick.shape[0]
    slots = entries // owned
    width = -(-(upsample.shape[1] + nodes) // 128) * 128
    return pl.pallas_call(
        near_kernel,
        grid_spec=pltpu.PrefetchScalarGridSpec(
            num_scalar_prefetch=2,
            grid=(owned, slots),
            in_specs=[whole(got), whole(upsample), whole(targets), whole(base)],
            out_specs=whole(targets),
            scratch_shapes=[
                pltpu.VMEM((entries, 8, nodes), f32),
                pltpu.VMEM((entries, 8, width), f32),
                pltpu.VMEM((80, nodes), f32),
                pltpu.VMEM((32, nodes), bf16),
            ],
        ),
        out_shape=jax.ShapeDtypeStruct(targets.shape, f32),
        name="near_pairs",
    )(counts, pick, got, upsample, targets, base)


def per_device(
    drop_points,
    drop_strength,
    upsample,
    base_velocity,
    near_drops,
    near_count,
    patch_points,
    patch_strength,
    wall_near,
):
    ranks = lax.axis_size("drops")
    walls = lax.axis_size("wall")
    owned, _, coarse = drop_points.shape
    slots = near_drops.shape[1]
    entries = owned * slots
    depth = max(2, (entries + ranks - 1) // ranks)
    here = lax.axis_index("wall")

    partner = near_drops.reshape(entries)
    owner = partner // owned % ranks
    local = partner % owned
    member = (owner[:, None] == jnp.arange(ranks, dtype=jnp.int32)[None, :]).astype(jnp.int32)
    position = jnp.sum((jnp.cumsum(member, axis=0) - 1) * member, axis=1)
    slot_hit = member[:, :, None] * (
        position[:, None, None] == jnp.arange(depth, dtype=jnp.int32)[None, None, :]
    ).astype(jnp.int32)
    requests = jnp.sum(slot_hit * local[:, None, None], axis=0)
    incoming = lax.all_to_all(requests, "drops", split_axis=0, concat_axis=0, tiled=True)

    both = jnp.concatenate([drop_points, drop_strength], axis=1)
    send = jnp.take(both, incoming.reshape(ranks * depth), axis=0)
    send = send.reshape(ranks, depth, 6, coarse).transpose(0, 2, 1, 3)

    held = patch_points.shape[0]
    listed = wall_near.shape[1]
    wanted, send = lax.optimization_barrier((wall_near.reshape(owned * listed), send))
    got = lax.all_to_all(send, "drops", split_axis=0, concat_axis=0, tiled=True)
    asked = [wanted]
    for r in range(1, walls):
        asked.append(lax.ppermute(wanted, "wall", [(w, (w + r) % walls) for w in range(walls)]))

    index = jnp.clip(jnp.concatenate(asked) - here * held, 0, held - 1)
    rows = jnp.concatenate(
        [jnp.take(patch_points, index, axis=0), jnp.take(patch_strength, index, axis=0)], axis=1
    )
    rows = rows.reshape(walls, owned * listed, -1)
    home = wanted // held
    mine = rows[0]
    for r in range(1, walls):
        back = lax.ppermute(rows[r], "wall", [(w, (w - r) % walls) for w in range(walls)])
        mine = jnp.where((home == (here + r) % walls)[:, None], back, mine)
    patch = rows.shape[2] // 6
    mine = mine.reshape(owned, listed, 6, patch).transpose(0, 2, 1, 3).reshape(owned, 6, -1)

    targets = drop_points.transpose(1, 0, 2)
    total = near_sums(
        near_count, owner * depth + position, got, upsample, targets, base_velocity.transpose(1, 0, 2)
    )
    total = wall_sums(mine, targets, total)
    return total.transpose(1, 0, 2)


def solution(mesh):
    return jax.shard_map(
        per_device,
        mesh=mesh,
        in_specs=(
            P(("wall", "drops"), None, None),
            P(("wall", "drops"), None, None),
            P(),
            P(("wall", "drops"), None, None),
            P(("wall", "drops"), None),
            P(("wall", "drops")),
            P("wall", None),
            P("wall", None),
            P(("wall", "drops"), None),
        ),
        out_specs=P(("wall", "drops"), None, None),
        check_vma=False,
    )
```

```python
import jax
import jax.numpy as jnp
from jax import lax
from jax.experimental import pallas as pl
from jax.experimental.pallas import tpu as pltpu
from jax.sharding import PartitionSpec as P


smoothing_square = 0.25
f32 = jnp.float32
bf16 = jnp.bfloat16


def nn(a, b):
    return jnp.dot(a, b, preferred_element_type=f32)


def split(v, count):
    out = []
    for left in reversed(range(count)):
        p = v.astype(bf16)
        out.append(p)
        if left:
            v = v - p.astype(f32)
    return out


def source_rows(row):
    y = [row(c) for c in range(3)]
    g = [row(3 + c) for c in range(3)]
    width = y[0].shape[1]
    y = [jnp.broadcast_to(v, (8, width)) for v in y]
    g = [jnp.broadcast_to(v, (8, width)) for v in g]
    at = lax.broadcasted_iota(jnp.int32, (8, width), 0)

    def lay(*values):
        out = values[-1]
        for r in range(len(values) - 2, -1, -1):
            if values[r] is not values[r + 1]:
                out = jnp.where(at <= r, values[r], out)
        return out

    one = jnp.ones((8, width), f32)
    zero = jnp.zeros((8, width), f32)
    square = y[0] * y[0] + y[1] * y[1] + y[2] * y[2]
    along = y[0] * g[0] + y[1] * g[1] + y[2] * g[2]
    grown = square + 2.0 * smoothing_square
    top = lay(g[0], g[1], g[2], g[0], g[1], g[2], g[0], g[1]) * lay(
        one, one, one, y[0], y[0], y[0], y[1], y[1]
    )
    low = lay(g[2], g[0], g[1], g[2], g[0], g[1], g[2], g[2]) * lay(
        y[1], y[2], y[2], y[2], grown, grown, grown, zero
    ) + along * lay(zero, zero, zero, zero, y[0], y[1], y[2], zero)
    c = split(jnp.concatenate([top, low], axis=0), 3)
    b = [p.astype(f32) for p in split(lay(y[0], y[1], y[2], square, y[0], y[1], y[2], square), 3)]
    first = jnp.where(at < 4, b[0], b[1])
    second = jnp.where(at < 4, b[2], one)
    dist = jnp.concatenate([first, second, first, b[0]], axis=0).astype(bf16)
    return dist, jnp.concatenate(c, axis=0), jnp.concatenate(c[:2], axis=0)


def target_rows(x):
    square = x[0] * x[0] + x[1] * x[1] + x[2] * x[2] + smoothing_square
    one = jnp.ones_like(square)
    zero = jnp.zeros_like(square)
    a = [split(-2.0 * v, 3) for v in x]
    a = [[p.astype(f32) for p in v] for v in a]
    s = [p.astype(f32) for p in split(square, 3)]
    top = [a[0][0], a[1][0], a[2][0], one]
    rows = top * 3 + s + [zero]
    rows += [a[0][1], a[1][1], a[2][1], zero] * 2
    rows += [a[0][2], a[1][2], a[2][2], zero] + [zero] * 4
    return jnp.concatenate(rows, axis=0).astype(bf16)


def accumulate(acc_ref, xf, row):
    dist_rows, three, two = source_rows(row)
    dist = lax.dot_general(dist_rows, xf, (((0,), (0,)), ((), ())), preferred_element_type=f32)
    w = lax.rsqrt(dist)
    w3 = w * w * w
    hi = w3.astype(bf16)
    lo = (w3 - hi.astype(f32)).astype(bf16)
    acc_ref[:48] += nn(three, hi)
    acc_ref[48:] += nn(two, lo)


def finish(acc_ref, t_ref, b_ref, o_ref, drop, rest=None):
    q = acc_ref[0:16] + acc_ref[16:32] + acc_ref[32:48] + (acc_ref[48:64] + acc_ref[64:80])
    at = pl.ds(drop, 1)
    x = [t_ref[i, at][:, : acc_ref.shape[1]] for i in range(3)]
    square = x[0] * x[0] + x[1] * x[1] + x[2] * x[2]
    gs = [q[a : a + 1] for a in range(3)]
    h = [[q[3 + 3 * b + a : 4 + 3 * b + a] for a in range(3)] for b in range(3)]
    m = [q[12 + a : 13 + a] for a in range(3)]
    lean = x[0] * gs[0] + x[1] * gs[1] + x[2] * gs[2] - (h[0][0] + h[1][1] + h[2][2])
    for a in range(3):
        u = m[a] + square * gs[a] + x[a] * lean
        for b in range(3):
            u = u - x[b] * (2.0 * h[b][a] + h[a][b])
        if rest is not None:
            u = jnp.concatenate([u, rest[a]], axis=1)
        o_ref[a, at] = b_ref[a, at] + u


def wall_kernel(wall_ref, t_ref, b_ref, o_ref, acc_ref):
    drop = pl.program_id(0)
    acc_ref[...] = jnp.zeros_like(acc_ref)
    xf = target_rows([t_ref[i, pl.ds(drop, 1)] for i in range(3)])
    accumulate(acc_ref, xf, lambda c: wall_ref[drop, c : c + 1])
    finish(acc_ref, t_ref, b_ref, o_ref, drop)


TILE = 256


def upsample_rows(high, low, up_ref, f_ref):
    depth, fine = up_ref.shape
    rows = high.shape[0]
    ks = range(0, depth, TILE)

    def padded(v, shape):
        for axis in range(2):
            if v.shape[axis] < shape[axis]:
                gap = list(v.shape)
                gap[axis] = shape[axis] - v.shape[axis]
                v = jnp.concatenate([v, jnp.zeros(gap, v.dtype)], axis=axis)
        return v

    parts = [
        [padded(v[:, k : min(k + TILE, depth)], (rows, TILE)) for k in ks] for v in (high, low)
    ]

    def body(*accs):
        pushed = [0, 0]

        def push(m, value):
            register = pushed[m] % 2
            pushed[m] += 1
            pltpu.matmul_push_rhs(value, staging_register=register, mxu_index=m)
            return register

        tiles = list(enumerate(range(0, fine, TILE)))

        def flush(i, n0):
            n1 = min(n0 + TILE, fine)
            f = pltpu.matmul_pop(accs[i % 4])[:, : n1 - n0]
            f_ref[:, :, n0:n1] = f.reshape(f_ref.shape[0], 8, n1 - n0)

        for i, n0 in tiles:
            m = i % 2
            n1 = min(n0 + TILE, fine)
            for j, k in enumerate(ks):
                up = split(up_ref[k : min(k + TILE, depth), n0:n1], 2)
                up = [padded(p, (TILE, TILE)) for p in up]
                register = push(m, up[0])
                pltpu.matmul_acc_lhs(accs[i % 4], parts[0][j], load_staged_rhs=register)
                pltpu.matmul_acc_lhs(accs[i % 4], parts[1][j])
                register = push(m, up[1])
                pltpu.matmul_acc_lhs(accs[i % 4], parts[0][j], load_staged_rhs=register)
            if i >= 2:
                flush(*tiles[i - 2])
        for tile in tiles[-2:]:
            flush(*tile)

    pl.run_scoped(body, *[pltpu.ACC(m)((rows, TILE), f32) for m in (0, 1, 0, 1)])


def near_slot(row, width, xp_ref, acc_ref, u_ref, xb_ref, w_ref):
    whole_chunks, half = divmod(width, TILE)
    units = range(2)
    cols = {}

    def body(*refs):
        main = [refs[0:3], refs[3:6]]
        tail, high, low = refs[6:8], refs[8:10], refs[10:12]
        pushed = [0, 0]

        def push(m, value):
            register = pushed[m] % 2
            pushed[m] += 1
            pltpu.matmul_push_rhs(value, staging_register=register, mxu_index=m)
            return register

        def start(chunks):
            lhs = []
            for c in chunks:
                size = TILE if c < whole_chunks else half
                dist, three, two = source_rows(lambda r: row(r, c * TILE, size))
                cols[c] = three, two
                turned = jnp.concatenate([dist, jnp.zeros((96, size), bf16)], axis=0).T
                lhs.append(jnp.concatenate([turned, jnp.zeros((size, 128), bf16)], axis=1))
            for m in units:
                register = push(m, xp_ref[m])
                for c, value in zip(chunks, lhs):
                    into = main[m][c % 3] if c < whole_chunks else tail[m]
                    pltpu.matmul_acc_lhs(into, value, load_staged_rhs=register)
                    register = None

        def cube(c, m):
            w = lax.rsqrt(pltpu.matmul_pop(main[m][c % 3] if c < whole_chunks else tail[m]))
            return split(w * w * w, 2)

        def keep(c, m):
            hi, lo = cube(c, m)
            w_ref[c % 2, m, 0] = hi
            w_ref[c % 2, m, 1] = lo

        def reduce(c, m):
            three, two = cols[c]
            register = push(m, w_ref[c % 2, m, 0])
            pltpu.matmul_acc_lhs(high[m], three, load_staged_rhs=register)
            register = push(m, w_ref[c % 2, m, 1])
            pltpu.matmul_acc_lhs(low[m], two, load_staged_rhs=register)

        last = whole_chunks + (1 if half else 0)
        start([0])
        for c in range(whole_chunks):
            if c % 2 == 0 and c + 1 < last:
                start([k for k in (c + 1, c + 2) if k < last])
            keep(c, 0)
            if c > 0:
                reduce(c - 1, 1)
            keep(c, 1)
            reduce(c, 0)
        reduce(whole_chunks - 1, 1)
        if half:
            three, two = cols[whole_chunks]
            two = jnp.concatenate([two, jnp.zeros((16, half), bf16)], axis=0)
            both = jnp.concatenate([three, two], axis=1)
            for m in units:
                hi, lo = cube(whole_chunks, m)
                register = push(m, jnp.concatenate([hi, lo], axis=0))
                pltpu.matmul_acc_lhs(high[m], both, load_staged_rhs=register)
        for m in units:
            at = slice(m * TILE, (m + 1) * TILE)
            acc_ref[:48, at] += pltpu.matmul_pop(high[m])
            acc_ref[48:, at] += pltpu.matmul_pop(low[m])

    acc = pltpu.ACC
    pl.run_scoped(
        body,
        *[acc(m)((TILE, TILE), f32) for m in (0, 0, 0, 1, 1, 1)],
        *[acc(m)((128, TILE), f32) for m in units],
        *[acc(m)((48, TILE), f32) for m in units],
        *[acc(m)((32, TILE), f32) for m in units],
    )

    x = [xb_ref[i] for i in range(3)]
    u = [u_ref[i] for i in range(3)]
    for s0 in range(0, width, 128):
        y = [row(i, s0, 128) for i in range(3)]
        g = [row(3 + i, s0, 128) for i in range(3)]
        d = [x[i] - y[i] for i in range(3)]
        r = d[0] * d[0] + d[1] * d[1] + d[2] * d[2] + smoothing_square
        w = lax.rsqrt(r)
        w3 = w * w * w
        along = (d[0] * g[0] + d[1] * g[1] + d[2] * g[2]) * w3
        plain = (r + smoothing_square) * w3
        u = [u[i] + (plain * g[i] + along * d[i]) for i in range(3)]
    for i in range(3):
        u_ref[i] = u[i]


def near_kernel(
    count_ref, pick_ref, got_ref, up_ref, t_ref, b_ref, o_ref,
    cbuf, f_ref, acc_ref, xp_ref, u_ref, xb_ref, w_ref,
):
    drop = pl.program_id(0)
    slot = pl.program_id(1)
    slots = pl.num_programs(1)
    entries = f_ref.shape[0]
    depth = got_ref.shape[2]
    coarse = got_ref.shape[3]
    fine = up_ref.shape[1]
    tiled = 2 * TILE
    rest = coarse - tiled

    @pl.when((drop == 0) & (slot == 0))
    def _():
        pad = jnp.zeros((2, coarse), f32)
        for e in range(entries):
            both = got_ref[pick_ref[e] // depth]
            place = pick_ref[e] % depth
            row = both[:, 0]
            for p in range(1, depth):
                row = jnp.where(place == p, both[:, p], row)
            cbuf[e] = jnp.concatenate([row, pad], axis=0)
        source = cbuf[...]
        high, low = split(source.reshape(entries * 8, coarse), 2)
        upsample_rows(high, low, up_ref, f_ref)
        tail = f_ref.shape[2] - fine - coarse
        at = lax.broadcasted_iota(jnp.int32, source.shape, 1)
        source = jnp.where(at < 3, source, -source)
        f_ref[:, :, fine:] = jnp.concatenate(
            [source, jnp.zeros((entries, 8, tail), f32)], axis=2
        )

        xp_ref[...] = jnp.zeros_like(xp_ref)

    @pl.when(slot == 0)
    def _():
        x = [t_ref[i, pl.ds(drop, 1)] for i in range(3)]
        feats = target_rows([v[:, :tiled] for v in x])
        for m in range(2):
            xp_ref[m, :32] = feats[:, m * TILE : (m + 1) * TILE]
        for i in range(3):
            end = jnp.concatenate([x[i][:, tiled:], jnp.zeros((1, 128 - rest), f32)], axis=1)
            xb_ref[i] = jnp.broadcast_to(end, (128, 128)).T[:rest]
        acc_ref[...] = jnp.zeros_like(acc_ref)
        u_ref[...] = jnp.zeros_like(u_ref)

    @pl.when(slot < count_ref[drop])
    def _():
        entry = drop * slots + slot
        near_slot(
            lambda c, s0, size: f_ref[entry, c : c + 1, s0 : s0 + size],
            f_ref.shape[2], xp_ref, acc_ref, u_ref, xb_ref, w_ref,
        )

    @pl.when(slot == slots - 1)
    def _():
        blank = jnp.zeros((128 - 3 * rest, 128), f32)
        sums = jnp.concatenate([u_ref[0], u_ref[1], u_ref[2], blank], axis=0).T
        line = jnp.sum(sums, axis=0, keepdims=True)
        ends = [line[:, i * rest : (i + 1) * rest] for i in range(3)]
        finish(acc_ref, t_ref, b_ref, o_ref, drop, ends)


def whole(a):
    zeros = (0,) * len(a.shape)
    return pl.BlockSpec(a.shape, lambda *_: zeros, pipeline_mode=pl.Buffered(1))


def wall_sums(wall, targets, base):
    _, owned, nodes = targets.shape
    return pl.pallas_call(
        wall_kernel,
        grid=(owned,),
        in_specs=[whole(wall), whole(targets), whole(base)],
        out_specs=whole(targets),
        scratch_shapes=[
            pltpu.VMEM((80, nodes), f32),
        ],
        out_shape=jax.ShapeDtypeStruct(targets.shape, f32),
        name="wall_pairs",
    )(wall, targets, base)


def near_sums(counts, pick, got, upsample, targets, base):
    _, owned, nodes = targets.shape
    entries = pick.shape[0]
    slots = entries // owned
    width = -(-(upsample.shape[1] + nodes) // 128) * 128
    return pl.pallas_call(
        near_kernel,
        grid_spec=pltpu.PrefetchScalarGridSpec(
            num_scalar_prefetch=2,
            grid=(owned, slots),
            in_specs=[whole(got), whole(upsample), whole(targets), whole(base)],
            out_specs=whole(targets),
            scratch_shapes=[
                pltpu.VMEM((entries, 8, nodes), f32),
                pltpu.VMEM((entries, 8, width), f32),
                pltpu.VMEM((80, 2 * TILE), f32),
                pltpu.VMEM((2, TILE, TILE), bf16),
                pltpu.VMEM((3, nodes - 2 * TILE, 128), f32),
                pltpu.VMEM((3, nodes - 2 * TILE, 128), f32),
                pltpu.VMEM((2, 2, 2, TILE, TILE), bf16),
            ],
        ),
        out_shape=jax.ShapeDtypeStruct(targets.shape, f32),
        name="near_pairs",
    )(counts, pick, got, upsample, targets, base)


def per_device(
    drop_points,
    drop_strength,
    upsample,
    base_velocity,
    near_drops,
    near_count,
    patch_points,
    patch_strength,
    wall_near,
):
    ranks = lax.axis_size("drops")
    walls = lax.axis_size("wall")
    owned, _, coarse = drop_points.shape
    slots = near_drops.shape[1]
    entries = owned * slots
    depth = max(2, (entries + ranks - 1) // ranks)
    here = lax.axis_index("wall")

    partner = near_drops.reshape(entries)
    owner = partner // owned % ranks
    local = partner % owned
    member = (owner[:, None] == jnp.arange(ranks, dtype=jnp.int32)[None, :]).astype(jnp.int32)
    position = jnp.sum((jnp.cumsum(member, axis=0) - 1) * member, axis=1)
    slot_hit = member[:, :, None] * (
        position[:, None, None] == jnp.arange(depth, dtype=jnp.int32)[None, None, :]
    ).astype(jnp.int32)
    requests = jnp.sum(slot_hit * local[:, None, None], axis=0)
    incoming = lax.all_to_all(requests, "drops", split_axis=0, concat_axis=0, tiled=True)

    both = jnp.concatenate([drop_points, drop_strength], axis=1)
    send = jnp.take(both, incoming.reshape(ranks * depth), axis=0)
    send = send.reshape(ranks, depth, 6, coarse).transpose(0, 2, 1, 3)

    held = patch_points.shape[0]
    listed = wall_near.shape[1]
    wanted, send = lax.optimization_barrier((wall_near.reshape(owned * listed), send))
    got = lax.all_to_all(send, "drops", split_axis=0, concat_axis=0, tiled=True)
    asked = [wanted]
    for r in range(1, walls):
        asked.append(lax.ppermute(wanted, "wall", [(w, (w + r) % walls) for w in range(walls)]))

    index = jnp.clip(jnp.concatenate(asked) - here * held, 0, held - 1)
    rows = jnp.concatenate(
        [jnp.take(patch_points, index, axis=0), jnp.take(patch_strength, index, axis=0)], axis=1
    )
    rows = rows.reshape(walls, owned * listed, -1)
    home = wanted // held
    mine = rows[0]
    for r in range(1, walls):
        back = lax.ppermute(rows[r], "wall", [(w, (w - r) % walls) for w in range(walls)])
        mine = jnp.where((home == (here + r) % walls)[:, None], back, mine)
    patch = rows.shape[2] // 6
    mine = mine.reshape(owned, listed, 6, patch).transpose(0, 2, 1, 3).reshape(owned, 6, -1)

    targets = drop_points.transpose(1, 0, 2)
    pick = owner * depth + position
    total = near_sums(near_count, pick, got, upsample, targets, base_velocity.transpose(1, 0, 2))
    total = wall_sums(mine, targets, total)
    return total.transpose(1, 0, 2)


def solution(mesh):
    return jax.shard_map(
        per_device,
        mesh=mesh,
        in_specs=(
            P(("wall", "drops"), None, None),
            P(("wall", "drops"), None, None),
            P(),
            P(("wall", "drops"), None, None),
            P(("wall", "drops"), None),
            P(("wall", "drops")),
            P("wall", None),
            P("wall", None),
            P(("wall", "drops"), None),
        ),
        out_specs=P(("wall", "drops"), None, None),
        check_vma=False,
    )
```

```python
import jax
import jax.numpy as jnp
from jax import lax
from jax.experimental import pallas as pl
from jax.experimental.pallas import tpu as pltpu
from jax.sharding import PartitionSpec as P


smoothing_square = 0.25
f32 = jnp.float32
bf16 = jnp.bfloat16


def nn(a, b):
    return jnp.dot(a, b, preferred_element_type=f32)


def split(v, count):
    out = []
    for left in reversed(range(count)):
        p = v.astype(bf16)
        out.append(p)
        if left:
            v = v - p.astype(f32)
    return out


def source_rows(row):
    y = [row(c) for c in range(3)]
    g = [row(3 + c) for c in range(3)]
    width = y[0].shape[1]
    y = [jnp.broadcast_to(v, (8, width)) for v in y]
    g = [jnp.broadcast_to(v, (8, width)) for v in g]
    at = lax.broadcasted_iota(jnp.int32, (8, width), 0)

    def lay(*values):
        out = values[-1]
        for r in range(len(values) - 2, -1, -1):
            if values[r] is not values[r + 1]:
                out = jnp.where(at <= r, values[r], out)
        return out

    one = jnp.ones((8, width), f32)
    zero = jnp.zeros((8, width), f32)
    square = y[0] * y[0] + y[1] * y[1] + y[2] * y[2]
    along = y[0] * g[0] + y[1] * g[1] + y[2] * g[2]
    grown = square + 2.0 * smoothing_square
    top = lay(g[0], g[1], g[2], g[0], g[1], g[2], g[0], g[1]) * lay(
        one, one, one, y[0], y[0], y[0], y[1], y[1]
    )
    low = lay(g[2], g[0], g[1], g[2], g[0], g[1], g[2], g[2]) * lay(
        y[1], y[2], y[2], y[2], grown, grown, grown, zero
    ) + along * lay(zero, zero, zero, zero, y[0], y[1], y[2], zero)
    c = split(jnp.concatenate([top, low], axis=0), 3)
    b = [p.astype(f32) for p in split(lay(y[0], y[1], y[2], square, y[0], y[1], y[2], square), 3)]
    first = jnp.where(at < 4, b[0], b[1])
    second = jnp.where(at < 4, b[2], one)
    dist = jnp.concatenate([first, second, first, b[0]], axis=0).astype(bf16)
    return dist, jnp.concatenate(c, axis=0), jnp.concatenate(c[:2], axis=0)


def target_rows(x):
    square = x[0] * x[0] + x[1] * x[1] + x[2] * x[2] + smoothing_square
    one = jnp.ones_like(square)
    zero = jnp.zeros_like(square)
    a = [split(-2.0 * v, 3) for v in x]
    a = [[p.astype(f32) for p in v] for v in a]
    s = [p.astype(f32) for p in split(square, 3)]
    top = [a[0][0], a[1][0], a[2][0], one]
    rows = top * 3 + s + [zero]
    rows += [a[0][1], a[1][1], a[2][1], zero] * 2
    rows += [a[0][2], a[1][2], a[2][2], zero] + [zero] * 4
    return jnp.concatenate(rows, axis=0).astype(bf16)


def accumulate(acc_ref, xf, row):
    dist_rows, three, two = source_rows(row)
    dist = lax.dot_general(dist_rows, xf, (((0,), (0,)), ((), ())), preferred_element_type=f32)
    w = lax.rsqrt(dist)
    w3 = w * w * w
    hi = w3.astype(bf16)
    lo = (w3 - hi.astype(f32)).astype(bf16)
    acc_ref[:48] += nn(three, hi)
    acc_ref[48:] += nn(two, lo)


def finish(acc_ref, t_ref, b_ref, o_ref, drop, rest=None):
    q = acc_ref[0:16] + acc_ref[16:32] + acc_ref[32:48] + (acc_ref[48:64] + acc_ref[64:80])
    at = pl.ds(drop, 1)
    x = [t_ref[i, at][:, : acc_ref.shape[1]] for i in range(3)]
    square = x[0] * x[0] + x[1] * x[1] + x[2] * x[2]
    gs = [q[a : a + 1] for a in range(3)]
    h = [[q[3 + 3 * b + a : 4 + 3 * b + a] for a in range(3)] for b in range(3)]
    m = [q[12 + a : 13 + a] for a in range(3)]
    lean = x[0] * gs[0] + x[1] * gs[1] + x[2] * gs[2] - (h[0][0] + h[1][1] + h[2][2])
    for a in range(3):
        u = m[a] + square * gs[a] + x[a] * lean
        for b in range(3):
            u = u - x[b] * (2.0 * h[b][a] + h[a][b])
        if rest is not None:
            u = jnp.concatenate([u, rest[a]], axis=1)
        o_ref[a, at] = b_ref[a, at] + u


def wall_kernel(wall_ref, t_ref, b_ref, o_ref, acc_ref):
    drop = pl.program_id(0)
    acc_ref[...] = jnp.zeros_like(acc_ref)
    xf = target_rows([t_ref[i, pl.ds(drop, 1)] for i in range(3)])
    accumulate(acc_ref, xf, lambda c: wall_ref[drop, c : c + 1])
    finish(acc_ref, t_ref, b_ref, o_ref, drop)


TILE = 256


def upsample_rows(high, low, up_ref, f_ref):
    depth, fine = up_ref.shape
    rows = high.shape[0]
    ks = range(0, depth, TILE)

    def padded(v, shape):
        for axis in range(2):
            if v.shape[axis] < shape[axis]:
                gap = list(v.shape)
                gap[axis] = shape[axis] - v.shape[axis]
                v = jnp.concatenate([v, jnp.zeros(gap, v.dtype)], axis=axis)
        return v

    parts = [
        [padded(v[:, k : min(k + TILE, depth)], (rows, TILE)) for k in ks] for v in (high, low)
    ]

    def body(*accs):
        pushed = [0, 0]

        def push(m, value):
            register = pushed[m] % 2
            pushed[m] += 1
            pltpu.matmul_push_rhs(value, staging_register=register, mxu_index=m)
            return register

        tiles = list(enumerate(range(0, fine, TILE)))

        def flush(i, n0):
            n1 = min(n0 + TILE, fine)
            f = pltpu.matmul_pop(accs[i % 4])[:, : n1 - n0]
            f_ref[:, :, n0:n1] = f.reshape(f_ref.shape[0], 8, n1 - n0)

        for i, n0 in tiles:
            m = i % 2
            n1 = min(n0 + TILE, fine)
            for j, k in enumerate(ks):
                up = split(up_ref[k : min(k + TILE, depth), n0:n1], 2)
                up = [padded(p, (TILE, TILE)) for p in up]
                register = push(m, up[0])
                pltpu.matmul_acc_lhs(accs[i % 4], parts[0][j], load_staged_rhs=register)
                pltpu.matmul_acc_lhs(accs[i % 4], parts[1][j])
                register = push(m, up[1])
                pltpu.matmul_acc_lhs(accs[i % 4], parts[0][j], load_staged_rhs=register)
            if i >= 2:
                flush(*tiles[i - 2])
        for tile in tiles[-2:]:
            flush(*tile)

    pl.run_scoped(body, *[pltpu.ACC(m)((rows, TILE), f32) for m in (0, 1, 0, 1)])


def near_slot(row, width, xp_ref, acc_ref, u_ref, xb_ref, w_ref):
    whole_chunks, half = divmod(width, TILE)
    units = range(2)
    cols = {}

    def body(*refs):
        main = [refs[0:3], refs[3:6]]
        tail, high, low = refs[6:8], refs[8:10], refs[10:12]
        pushed = [0, 0]

        def push(m, value):
            register = pushed[m] % 2
            pushed[m] += 1
            pltpu.matmul_push_rhs(value, staging_register=register, mxu_index=m)
            return register

        def start(chunks):
            lhs = []
            for c in chunks:
                size = TILE if c < whole_chunks else half
                dist, three, two = source_rows(lambda r: row(r, c * TILE, size))
                cols[c] = three, two
                turned = jnp.concatenate([dist, jnp.zeros((96, size), bf16)], axis=0).T
                lhs.append(jnp.concatenate([turned, jnp.zeros((size, 128), bf16)], axis=1))
            for m in units:
                register = push(m, xp_ref[m])
                for c, value in zip(chunks, lhs):
                    into = main[m][c % 3] if c < whole_chunks else tail[m]
                    pltpu.matmul_acc_lhs(into, value, load_staged_rhs=register)
                    register = None

        def cube(c, m):
            w = lax.rsqrt(pltpu.matmul_pop(main[m][c % 3] if c < whole_chunks else tail[m]))
            return split(w * w * w, 2)

        def keep(c, m):
            hi, lo = cube(c, m)
            w_ref[c % 2, m, 0] = hi
            w_ref[c % 2, m, 1] = lo

        def reduce(c, m):
            three, two = cols[c]
            register = push(m, w_ref[c % 2, m, 0])
            pltpu.matmul_acc_lhs(high[m], three, load_staged_rhs=register)
            register = push(m, w_ref[c % 2, m, 1])
            pltpu.matmul_acc_lhs(low[m], two, load_staged_rhs=register)

        last = whole_chunks + (1 if half else 0)
        start([0])
        for c in range(whole_chunks):
            if c % 2 == 0 and c + 1 < last:
                start([k for k in (c + 1, c + 2) if k < last])
            keep(c, 0)
            if c > 0:
                reduce(c - 1, 1)
            keep(c, 1)
            reduce(c, 0)
        reduce(whole_chunks - 1, 1)
        if half:
            three, two = cols[whole_chunks]
            two = jnp.concatenate([two, jnp.zeros((16, half), bf16)], axis=0)
            both = jnp.concatenate([three, two], axis=1)
            for m in units:
                hi, lo = cube(whole_chunks, m)
                register = push(m, jnp.concatenate([hi, lo], axis=0))
                pltpu.matmul_acc_lhs(high[m], both, load_staged_rhs=register)
        for m in units:
            at = slice(m * TILE, (m + 1) * TILE)
            acc_ref[:48, at] += pltpu.matmul_pop(high[m])
            acc_ref[48:, at] += pltpu.matmul_pop(low[m])

    acc = pltpu.ACC
    pl.run_scoped(
        body,
        *[acc(m)((TILE, TILE), f32) for m in (0, 0, 0, 1, 1, 1)],
        *[acc(m)((128, TILE), f32) for m in units],
        *[acc(m)((48, TILE), f32) for m in units],
        *[acc(m)((32, TILE), f32) for m in units],
    )

    x = [xb_ref[i] for i in range(3)]
    u = [u_ref[i] for i in range(3)]
    for s0 in range(0, width, 128):
        y = [row(i, s0, 128) for i in range(3)]
        g = [row(3 + i, s0, 128) for i in range(3)]
        d = [x[i] - y[i] for i in range(3)]
        r = d[0] * d[0] + d[1] * d[1] + d[2] * d[2] + smoothing_square
        w = lax.rsqrt(r)
        w3 = w * w * w
        along = (d[0] * g[0] + d[1] * g[1] + d[2] * g[2]) * w3
        plain = (r + smoothing_square) * w3
        u = [u[i] + (plain * g[i] + along * d[i]) for i in range(3)]
    for i in range(3):
        u_ref[i] = u[i]


def near_kernel(
    count_ref, pick_ref, got_ref, up_ref, t_ref, b_ref, o_ref,
    cbuf, f_ref, acc_ref, xp_ref, u_ref, xb_ref, w_ref,
):
    drop = pl.program_id(0)
    slot = pl.program_id(1)
    slots = pl.num_programs(1)
    entries = f_ref.shape[0]
    depth = got_ref.shape[2]
    coarse = got_ref.shape[3]
    fine = up_ref.shape[1]
    tiled = 2 * TILE
    rest = coarse - tiled

    @pl.when((drop == 0) & (slot == 0))
    def _():
        pad = jnp.zeros((2, coarse), f32)
        for e in range(entries):
            both = got_ref[pick_ref[e] // depth]
            place = pick_ref[e] % depth
            row = both[:, 0]
            for p in range(1, depth):
                row = jnp.where(place == p, both[:, p], row)
            cbuf[e] = jnp.concatenate([row, pad], axis=0)
        source = cbuf[...]
        high, low = split(source.reshape(entries * 8, coarse), 2)
        upsample_rows(high, low, up_ref, f_ref)
        tail = f_ref.shape[2] - fine - coarse
        at = lax.broadcasted_iota(jnp.int32, source.shape, 1)
        source = jnp.where(at < 3, source, -source)
        f_ref[:, :, fine:] = jnp.concatenate(
            [source, jnp.zeros((entries, 8, tail), f32)], axis=2
        )

        xp_ref[...] = jnp.zeros_like(xp_ref)

    @pl.when(slot == 0)
    def _():
        x = [t_ref[i, pl.ds(drop, 1)] for i in range(3)]
        feats = target_rows([v[:, :tiled] for v in x])
        for m in range(2):
            xp_ref[m, :32] = feats[:, m * TILE : (m + 1) * TILE]
        for i in range(3):
            end = jnp.concatenate([x[i][:, tiled:], jnp.zeros((1, 128 - rest), f32)], axis=1)
            xb_ref[i] = jnp.broadcast_to(end, (128, 128)).T[:rest]
        acc_ref[...] = jnp.zeros_like(acc_ref)
        u_ref[...] = jnp.zeros_like(u_ref)

    @pl.when(slot < count_ref[drop])
    def _():
        entry = drop * slots + slot
        near_slot(
            lambda c, s0, size: f_ref[entry, c : c + 1, s0 : s0 + size],
            f_ref.shape[2], xp_ref, acc_ref, u_ref, xb_ref, w_ref,
        )

    @pl.when(slot == slots - 1)
    def _():
        blank = jnp.zeros((128 - 3 * rest, 128), f32)
        sums = jnp.concatenate([u_ref[0], u_ref[1], u_ref[2], blank], axis=0).T
        line = jnp.sum(sums, axis=0, keepdims=True)
        ends = [line[:, i * rest : (i + 1) * rest] for i in range(3)]
        finish(acc_ref, t_ref, b_ref, o_ref, drop, ends)


def whole(a):
    zeros = (0,) * len(a.shape)
    return pl.BlockSpec(a.shape, lambda *_: zeros, pipeline_mode=pl.Buffered(1))


def wall_sums(wall, targets, base):
    _, owned, nodes = targets.shape
    return pl.pallas_call(
        wall_kernel,
        grid=(owned,),
        in_specs=[whole(wall), whole(targets), whole(base)],
        out_specs=whole(targets),
        scratch_shapes=[
            pltpu.VMEM((80, nodes), f32),
        ],
        out_shape=jax.ShapeDtypeStruct(targets.shape, f32),
        name="wall_pairs",
    )(wall, targets, base)


def near_sums(counts, pick, got, upsample, targets, base):
    _, owned, nodes = targets.shape
    entries = pick.shape[0]
    slots = entries // owned
    width = -(-(upsample.shape[1] + nodes) // 128) * 128
    return pl.pallas_call(
        near_kernel,
        grid_spec=pltpu.PrefetchScalarGridSpec(
            num_scalar_prefetch=2,
            grid=(owned, slots),
            in_specs=[whole(got), whole(upsample), whole(targets), whole(base)],
            out_specs=whole(targets),
            scratch_shapes=[
                pltpu.VMEM((entries, 8, nodes), f32),
                pltpu.VMEM((entries, 8, width), f32),
                pltpu.VMEM((80, 2 * TILE), f32),
                pltpu.VMEM((2, TILE, TILE), bf16),
                pltpu.VMEM((3, nodes - 2 * TILE, 128), f32),
                pltpu.VMEM((3, nodes - 2 * TILE, 128), f32),
                pltpu.VMEM((2, 2, 2, TILE, TILE), bf16),
            ],
        ),
        out_shape=jax.ShapeDtypeStruct(targets.shape, f32),
        name="near_pairs",
    )(counts, pick, got, upsample, targets, base)


def request_kernel(near_ref, ask_ref, pick_ref, seen_ref):
    ranks, _, depth = ask_ref.shape
    owned, slots = near_ref.shape
    for r in range(ranks):
        seen_ref[r] = 0
        for p in range(depth):
            ask_ref[r, 0, p] = 0
    for e in range(owned * slots):
        partner = near_ref[e // slots, e % slots]
        owner = partner // owned % ranks
        place = seen_ref[owner]
        seen_ref[owner] = place + 1
        ask_ref[owner, 0, place] = partner % owned
        pick_ref[e] = owner * depth + place


def make_requests(near_drops, ranks, depth):
    owned, slots = near_drops.shape
    smem = pl.BlockSpec(memory_space=pltpu.SMEM)
    return pl.pallas_call(
        request_kernel,
        in_specs=[smem],
        out_specs=[smem, smem],
        out_shape=[
            jax.ShapeDtypeStruct((ranks, 1, depth), jnp.int32),
            jax.ShapeDtypeStruct((owned * slots,), jnp.int32),
        ],
        scratch_shapes=[pltpu.SMEM((ranks,), jnp.int32)],
        name="requests",
    )(near_drops)


def send_kernel(ask_ref, pts_ref, str_ref, o_ref):
    ranks, _, depth, _ = o_ref.shape
    for r in range(ranks):
        for p in range(depth):
            at = pl.ds(ask_ref[r, 0, p], 1)
            o_ref[r, 0:3, p : p + 1] = pts_ref[:, at]
            o_ref[r, 3:6, p : p + 1] = str_ref[:, at]


def gather_drops(incoming, points, strength):
    ranks, _, depth = incoming.shape
    shape = (ranks, 6, depth, points.shape[2])
    return pl.pallas_call(
        send_kernel,
        grid_spec=pltpu.PrefetchScalarGridSpec(
            num_scalar_prefetch=1,
            grid=(1,),
            in_specs=[whole(points), whole(strength)],
            out_specs=pl.BlockSpec(shape, lambda *_: (0,) * 4, pipeline_mode=pl.Buffered(1)),
        ),
        out_shape=jax.ShapeDtypeStruct(shape, f32),
        name="send_rows",
    )(incoming, points, strength)


def patch_kernel(index_ref, pts_ref, str_ref, *outs):
    held = pts_ref.shape[1]
    count = index_ref.shape[1]
    step = 512
    index = jnp.broadcast_to(index_ref[...], (step, count))
    total = None
    for k in range(0, held, step):
        place = lax.broadcasted_iota(jnp.int32, (step, count), 0) + k
        hot = jnp.where(place == index, 1.0, 0.0).astype(bf16)
        rows = jnp.concatenate([pts_ref[:, k : k + step], str_ref[:, k : k + step]], axis=0)
        part = [nn(p, hot) for p in split(rows, 3)]
        part = part[0] + part[1] + part[2]
        total = part if total is None else total + part
    total = total.T
    each = outs[0].shape[0]
    for r, out in enumerate(outs):
        out[...] = total[r * each : (r + 1) * each]


def gather_patches(index, points, strength, walls):
    n = index.shape[1] // walls
    shape = jax.ShapeDtypeStruct((n, 2 * points.shape[0]), f32)
    return pl.pallas_call(
        patch_kernel,
        in_specs=[whole(index), whole(points), whole(strength)],
        out_specs=[whole(shape)] * walls,
        out_shape=[shape] * walls,
        name="patch_rows",
    )(index, points, strength)


def per_device(
    drop_points,
    drop_strength,
    upsample,
    base_velocity,
    near_drops,
    near_count,
    patch_points,
    patch_strength,
    wall_near,
):
    ranks = lax.axis_size("drops")
    walls = lax.axis_size("wall")
    owned, _, _ = drop_points.shape
    slots = near_drops.shape[1]
    entries = owned * slots
    depth = max(2, (entries + ranks - 1) // ranks)
    here = lax.axis_index("wall")

    targets = drop_points.transpose(1, 0, 2)

    requests, pick = make_requests(near_drops, ranks, depth)
    incoming = lax.all_to_all(requests, "drops", split_axis=0, concat_axis=0, tiled=True)
    send = gather_drops(incoming, targets, drop_strength.transpose(1, 0, 2))

    held = patch_points.shape[0]
    listed = wall_near.shape[1]
    wanted = wall_near.reshape(owned * listed)
    got = lax.all_to_all(send, "drops", split_axis=0, concat_axis=0, tiled=True)
    asked = [wanted]
    for r in range(1, walls):
        asked.append(lax.ppermute(wanted, "wall", [(w, (w + r) % walls) for w in range(walls)]))

    index = (jnp.concatenate(asked) - here * held)[None]
    rows = gather_patches(index, patch_points.T, patch_strength.T, walls)
    mine = rows[0]
    for r in range(1, walls):
        back = lax.ppermute(rows[r], "wall", [(w, (w - r) % walls) for w in range(walls)])
        mine = mine + back
    patch = mine.shape[1] // 6
    mine = mine.reshape(owned, listed, 6, patch).transpose(0, 2, 1, 3).reshape(owned, 6, -1)

    total = near_sums(near_count, pick, got, upsample, targets, base_velocity.transpose(1, 0, 2))
    total = wall_sums(mine, targets, total)
    return total.transpose(1, 0, 2)


def solution(mesh):
    return jax.shard_map(
        per_device,
        mesh=mesh,
        in_specs=(
            P(("wall", "drops"), None, None),
            P(("wall", "drops"), None, None),
            P(),
            P(("wall", "drops"), None, None),
            P(("wall", "drops"), None),
            P(("wall", "drops")),
            P("wall", None),
            P("wall", None),
            P(("wall", "drops"), None),
        ),
        out_specs=P(("wall", "drops"), None, None),
        check_vma=False,
    )
```

```python
import jax
import jax.numpy as jnp
from jax import lax
from jax.experimental import pallas as pl
from jax.experimental.pallas import tpu as pltpu
from jax.sharding import PartitionSpec as P


smoothing_square = 0.25
f32 = jnp.float32
bf16 = jnp.bfloat16


def nn(a, b):
    return jnp.dot(a, b, preferred_element_type=f32)


def split(v, count):
    out = []
    for left in reversed(range(count)):
        p = v.astype(bf16)
        out.append(p)
        if left:
            v = v - p.astype(f32)
    return out


def source_rows(row):
    y = [row(c) for c in range(3)]
    g = [row(3 + c) for c in range(3)]
    width = y[0].shape[1]
    y = [jnp.broadcast_to(v, (8, width)) for v in y]
    g = [jnp.broadcast_to(v, (8, width)) for v in g]
    at = lax.broadcasted_iota(jnp.int32, (8, width), 0)

    def lay(*values):
        out = values[-1]
        for r in range(len(values) - 2, -1, -1):
            if values[r] is not values[r + 1]:
                out = jnp.where(at <= r, values[r], out)
        return out

    one = jnp.ones((8, width), f32)
    zero = jnp.zeros((8, width), f32)
    square = y[0] * y[0] + y[1] * y[1] + y[2] * y[2]
    along = y[0] * g[0] + y[1] * g[1] + y[2] * g[2]
    grown = square + 2.0 * smoothing_square
    top = lay(g[0], g[1], g[2], g[0], g[1], g[2], g[0], g[1]) * lay(
        one, one, one, y[0], y[0], y[0], y[1], y[1]
    )
    low = lay(g[2], g[0], g[1], g[2], g[0], g[1], g[2], g[2]) * lay(
        y[1], y[2], y[2], y[2], grown, grown, grown, zero
    ) + along * lay(zero, zero, zero, zero, y[0], y[1], y[2], zero)
    c = split(jnp.concatenate([top, low], axis=0), 3)
    b = [p.astype(f32) for p in split(lay(y[0], y[1], y[2], square, y[0], y[1], y[2], square), 3)]
    first = jnp.where(at < 4, b[0], b[1])
    second = jnp.where(at < 4, b[2], one)
    dist = jnp.concatenate([first, second, first, b[0]], axis=0).astype(bf16)
    return dist, jnp.concatenate(c, axis=0), jnp.concatenate(c[:2], axis=0)


def target_rows(x):
    square = x[0] * x[0] + x[1] * x[1] + x[2] * x[2] + smoothing_square
    one = jnp.ones_like(square)
    zero = jnp.zeros_like(square)
    a = [split(-2.0 * v, 3) for v in x]
    a = [[p.astype(f32) for p in v] for v in a]
    s = [p.astype(f32) for p in split(square, 3)]
    top = [a[0][0], a[1][0], a[2][0], one]
    rows = top * 3 + s + [zero]
    rows += [a[0][1], a[1][1], a[2][1], zero] * 2
    rows += [a[0][2], a[1][2], a[2][2], zero] + [zero] * 4
    return jnp.concatenate(rows, axis=0).astype(bf16)


def finish(acc_ref, u_ref, t_ref, b_ref, o_ref, drop):
    rest = u_ref.shape[1]
    blank = jnp.zeros((128 - 3 * rest, 128), f32)
    sums = jnp.concatenate([u_ref[0], u_ref[1], u_ref[2], blank], axis=0).T
    line = jnp.sum(sums, axis=0, keepdims=True)
    q = acc_ref[0:16] + acc_ref[16:32] + acc_ref[32:48] + (acc_ref[48:64] + acc_ref[64:80])
    at = pl.ds(drop, 1)
    x = [t_ref[i, at][:, : acc_ref.shape[1]] for i in range(3)]
    square = x[0] * x[0] + x[1] * x[1] + x[2] * x[2]
    gs = [q[a : a + 1] for a in range(3)]
    h = [[q[3 + 3 * b + a : 4 + 3 * b + a] for a in range(3)] for b in range(3)]
    m = [q[12 + a : 13 + a] for a in range(3)]
    lean = x[0] * gs[0] + x[1] * gs[1] + x[2] * gs[2] - (h[0][0] + h[1][1] + h[2][2])
    for a in range(3):
        u = m[a] + square * gs[a] + x[a] * lean
        for b in range(3):
            u = u - x[b] * (2.0 * h[b][a] + h[a][b])
        u = jnp.concatenate([u, line[:, a * rest : (a + 1) * rest]], axis=1)
        o_ref[a, at] = b_ref[a, at] + u


TILE = 256


def upsample_rows(high, low, up_ref, f_ref):
    depth, fine = up_ref.shape
    rows = high.shape[0]
    ks = range(0, depth, TILE)

    def padded(v, shape):
        for axis in range(2):
            if v.shape[axis] < shape[axis]:
                gap = list(v.shape)
                gap[axis] = shape[axis] - v.shape[axis]
                v = jnp.concatenate([v, jnp.zeros(gap, v.dtype)], axis=axis)
        return v

    parts = [
        [padded(v[:, k : min(k + TILE, depth)], (rows, TILE)) for k in ks] for v in (high, low)
    ]

    def body(*accs):
        pushed = [0, 0]

        def push(m, value):
            register = pushed[m] % 2
            pushed[m] += 1
            pltpu.matmul_push_rhs(value, staging_register=register, mxu_index=m)
            return register

        tiles = list(enumerate(range(0, fine, TILE)))

        def flush(i, n0):
            n1 = min(n0 + TILE, fine)
            f = pltpu.matmul_pop(accs[i % 4])[:, : n1 - n0]
            f_ref[:, :, n0:n1] = f.reshape(f_ref.shape[0], 8, n1 - n0)

        for i, n0 in tiles:
            m = i % 2
            n1 = min(n0 + TILE, fine)
            for j, k in enumerate(ks):
                up = split(up_ref[k : min(k + TILE, depth), n0:n1], 2)
                up = [padded(p, (TILE, TILE)) for p in up]
                register = push(m, up[0])
                pltpu.matmul_acc_lhs(accs[i % 4], parts[0][j], load_staged_rhs=register)
                pltpu.matmul_acc_lhs(accs[i % 4], parts[1][j])
                register = push(m, up[1])
                pltpu.matmul_acc_lhs(accs[i % 4], parts[0][j], load_staged_rhs=register)
            if i >= 2:
                flush(*tiles[i - 2])
        for tile in tiles[-2:]:
            flush(*tile)

    pl.run_scoped(body, *[pltpu.ACC(m)((rows, TILE), f32) for m in (0, 1, 0, 1)])


def near_slot(row, width, xp_ref, acc_ref, u_ref, xb_ref, w_ref):
    whole_chunks, half = divmod(width, TILE)
    units = range(2)
    cols = {}

    def body(*refs):
        main = [refs[0:3], refs[3:6]]
        tail, high, low = refs[6:8], refs[8:10], refs[10:12]
        pushed = [0, 0]

        def push(m, value):
            register = pushed[m] % 2
            pushed[m] += 1
            pltpu.matmul_push_rhs(value, staging_register=register, mxu_index=m)
            return register

        def start(chunks):
            lhs = []
            for c in chunks:
                size = TILE if c < whole_chunks else half
                dist, three, two = source_rows(lambda r: row(r, c * TILE, size))
                cols[c] = three, two
                turned = jnp.concatenate([dist, jnp.zeros((96, size), bf16)], axis=0).T
                lhs.append(jnp.concatenate([turned, jnp.zeros((size, 128), bf16)], axis=1))
            for m in units:
                register = push(m, xp_ref[m])
                for c, value in zip(chunks, lhs):
                    into = main[m][c % 3] if c < whole_chunks else tail[m]
                    pltpu.matmul_acc_lhs(into, value, load_staged_rhs=register)
                    register = None

        def cube(c, m):
            w = lax.rsqrt(pltpu.matmul_pop(main[m][c % 3] if c < whole_chunks else tail[m]))
            return split(w * w * w, 2)

        def keep(c, m):
            hi, lo = cube(c, m)
            w_ref[c % 2, m, 0] = hi
            w_ref[c % 2, m, 1] = lo

        def reduce(c, m):
            three, two = cols[c]
            register = push(m, w_ref[c % 2, m, 0])
            pltpu.matmul_acc_lhs(high[m], three, load_staged_rhs=register)
            register = push(m, w_ref[c % 2, m, 1])
            pltpu.matmul_acc_lhs(low[m], two, load_staged_rhs=register)

        last = whole_chunks + (1 if half else 0)
        start([0])
        for c in range(whole_chunks):
            if c % 2 == 0 and c + 1 < last:
                start([k for k in (c + 1, c + 2) if k < last])
            keep(c, 0)
            if c > 0:
                reduce(c - 1, 1)
            keep(c, 1)
            reduce(c, 0)
        reduce(whole_chunks - 1, 1)
        if half:
            three, two = cols[whole_chunks]
            two = jnp.concatenate([two, jnp.zeros((16, half), bf16)], axis=0)
            both = jnp.concatenate([three, two], axis=1)
            for m in units:
                hi, lo = cube(whole_chunks, m)
                register = push(m, jnp.concatenate([hi, lo], axis=0))
                pltpu.matmul_acc_lhs(high[m], both, load_staged_rhs=register)
        for m in units:
            at = slice(m * TILE, (m + 1) * TILE)
            acc_ref[:48, at] += pltpu.matmul_pop(high[m])
            acc_ref[48:, at] += pltpu.matmul_pop(low[m])

    acc = pltpu.ACC
    pl.run_scoped(
        body,
        *[acc(m)((TILE, TILE), f32) for m in (0, 0, 0, 1, 1, 1)],
        *[acc(m)((128, TILE), f32) for m in units],
        *[acc(m)((48, TILE), f32) for m in units],
        *[acc(m)((32, TILE), f32) for m in units],
    )

    x = [xb_ref[i] for i in range(3)]
    u = [u_ref[i] for i in range(3)]
    for s0 in range(0, width, 128):
        y = [row(i, s0, 128) for i in range(3)]
        g = [row(3 + i, s0, 128) for i in range(3)]
        d = [x[i] - y[i] for i in range(3)]
        r = d[0] * d[0] + d[1] * d[1] + d[2] * d[2] + smoothing_square
        w = lax.rsqrt(r)
        w3 = w * w * w
        along = (d[0] * g[0] + d[1] * g[1] + d[2] * g[2]) * w3
        plain = (r + smoothing_square) * w3
        u = [u[i] + (plain * g[i] + along * d[i]) for i in range(3)]
    for i in range(3):
        u_ref[i] = u[i]


def set_targets(drop, t_ref, xp_ref, acc_ref, u_ref, xb_ref):
    tiled = 2 * TILE
    x = [t_ref[i, pl.ds(drop, 1)] for i in range(3)]
    feats = target_rows([v[:, :tiled] for v in x])
    for m in range(2):
        xp_ref[m, :32] = feats[:, m * TILE : (m + 1) * TILE]
    rest = xb_ref.shape[1]
    for i in range(3):
        end = jnp.concatenate([x[i][:, tiled:], jnp.zeros((1, 128 - rest), f32)], axis=1)
        xb_ref[i] = jnp.broadcast_to(end, (128, 128)).T[:rest]
    acc_ref[...] = jnp.zeros_like(acc_ref)
    u_ref[...] = jnp.zeros_like(u_ref)


def wall_kernel(wall_ref, t_ref, b_ref, o_ref, acc_ref, xp_ref, u_ref, xb_ref, w_ref):
    xp_ref[...] = jnp.zeros_like(xp_ref)

    def one_drop(drop, carry):
        set_targets(drop, t_ref, xp_ref, acc_ref, u_ref, xb_ref)
        near_slot(
            lambda c, s0, size: wall_ref[drop, c : c + 1, s0 : s0 + size],
            wall_ref.shape[2], xp_ref, acc_ref, u_ref, xb_ref, w_ref,
        )
        finish(acc_ref, u_ref, t_ref, b_ref, o_ref, drop)
        return carry

    lax.fori_loop(0, t_ref.shape[1], one_drop, 0)


def near_kernel(
    count_ref, pick_ref, got_ref, up_ref, t_ref, b_ref, o_ref,
    cbuf, f_ref, acc_ref, xp_ref, u_ref, xb_ref, w_ref,
):
    entries = f_ref.shape[0]
    owned = t_ref.shape[1]
    slots = entries // owned
    depth = got_ref.shape[2]
    coarse = got_ref.shape[3]
    fine = up_ref.shape[1]

    @pl.when(count_ref[0] >= 0)
    def _():
        pad = jnp.zeros((2, coarse), f32)
        for e in range(entries):
            both = got_ref[pick_ref[e] // depth]
            place = pick_ref[e] % depth
            row = both[:, 0]
            for p in range(1, depth):
                row = jnp.where(place == p, both[:, p], row)
            cbuf[e] = jnp.concatenate([row, pad], axis=0)
        source = cbuf[...]
        high, low = split(source.reshape(entries * 8, coarse), 2)
        upsample_rows(high, low, up_ref, f_ref)
        tail = f_ref.shape[2] - fine - coarse
        at = lax.broadcasted_iota(jnp.int32, source.shape, 1)
        source = jnp.where(at < 3, source, -source)
        f_ref[:, :, fine:] = jnp.concatenate(
            [source, jnp.zeros((entries, 8, tail), f32)], axis=2
        )

    xp_ref[...] = jnp.zeros_like(xp_ref)

    def one_drop(drop, carry):
        set_targets(drop, t_ref, xp_ref, acc_ref, u_ref, xb_ref)

        def one_slot(slot, inner):
            entry = drop * slots + slot
            near_slot(
                lambda c, s0, size: f_ref[entry, c : c + 1, s0 : s0 + size],
                f_ref.shape[2], xp_ref, acc_ref, u_ref, xb_ref, w_ref,
            )
            return inner

        lax.fori_loop(0, count_ref[drop], one_slot, 0)
        finish(acc_ref, u_ref, t_ref, b_ref, o_ref, drop)
        return carry

    lax.fori_loop(0, owned, one_drop, 0)


def whole(a):
    zeros = (0,) * len(a.shape)
    return pl.BlockSpec(a.shape, lambda *_: zeros, pipeline_mode=pl.Buffered(1))


def sum_scratch(nodes):
    return [
        pltpu.VMEM((80, 2 * TILE), f32),
        pltpu.VMEM((2, TILE, TILE), bf16),
        pltpu.VMEM((3, nodes - 2 * TILE, 128), f32),
        pltpu.VMEM((3, nodes - 2 * TILE, 128), f32),
        pltpu.VMEM((2, 2, 2, TILE, TILE), bf16),
    ]


def wall_sums(wall, targets, base):
    return pl.pallas_call(
        wall_kernel,
        in_specs=[whole(wall), whole(targets), whole(base)],
        out_specs=whole(targets),
        scratch_shapes=sum_scratch(targets.shape[2]),
        out_shape=jax.ShapeDtypeStruct(targets.shape, f32),
        name="wall_pairs",
    )(wall, targets, base)


def near_sums(counts, pick, got, upsample, targets, base):
    nodes = targets.shape[2]
    entries = pick.shape[0]
    width = -(-(upsample.shape[1] + nodes) // 128) * 128
    smem = pl.BlockSpec(memory_space=pltpu.SMEM)
    return pl.pallas_call(
        near_kernel,
        in_specs=[smem, smem, whole(got), whole(upsample), whole(targets), whole(base)],
        out_specs=whole(targets),
        scratch_shapes=[
            pltpu.VMEM((entries, 8, nodes), f32),
            pltpu.VMEM((entries, 8, width), f32),
            *sum_scratch(nodes),
        ],
        out_shape=jax.ShapeDtypeStruct(targets.shape, f32),
        name="near_pairs",
    )(counts, pick, got, upsample, targets, base)


def request_kernel(near_ref, ask_ref, pick_ref, seen_ref):
    ranks, _, depth = ask_ref.shape
    owned, slots = near_ref.shape
    for r in range(ranks):
        seen_ref[r] = 0
        for p in range(depth):
            ask_ref[r, 0, p] = 0
    for e in range(owned * slots):
        partner = near_ref[e // slots, e % slots]
        owner = partner // owned % ranks
        place = seen_ref[owner]
        seen_ref[owner] = place + 1
        ask_ref[owner, 0, place] = partner % owned
        pick_ref[e] = owner * depth + place


def make_requests(near_drops, ranks, depth):
    owned, slots = near_drops.shape
    smem = pl.BlockSpec(memory_space=pltpu.SMEM)
    return pl.pallas_call(
        request_kernel,
        in_specs=[smem],
        out_specs=[smem, smem],
        out_shape=[
            jax.ShapeDtypeStruct((ranks, 1, depth), jnp.int32),
            jax.ShapeDtypeStruct((owned * slots,), jnp.int32),
        ],
        scratch_shapes=[pltpu.SMEM((ranks,), jnp.int32)],
        name="requests",
    )(near_drops)


def send_kernel(ask_ref, pts_ref, str_ref, o_ref):
    ranks, _, depth, _ = o_ref.shape
    for r in range(ranks):
        for p in range(depth):
            at = pl.ds(ask_ref[r, 0, p], 1)
            o_ref[r, 0:3, p : p + 1] = pts_ref[:, at]
            o_ref[r, 3:6, p : p + 1] = str_ref[:, at]


def gather_drops(incoming, points, strength):
    ranks, _, depth = incoming.shape
    shape = (ranks, 6, depth, points.shape[2])
    return pl.pallas_call(
        send_kernel,
        grid_spec=pltpu.PrefetchScalarGridSpec(
            num_scalar_prefetch=1,
            grid=(1,),
            in_specs=[whole(points), whole(strength)],
            out_specs=pl.BlockSpec(shape, lambda *_: (0,) * 4, pipeline_mode=pl.Buffered(1)),
        ),
        out_shape=jax.ShapeDtypeStruct(shape, f32),
        name="send_rows",
    )(incoming, points, strength)


def patch_kernel(index_ref, pts_ref, str_ref, *outs):
    held = pts_ref.shape[1]
    count = index_ref.shape[1]
    step = 512
    index = jnp.broadcast_to(index_ref[...], (step, count))
    total = None
    for k in range(0, held, step):
        place = lax.broadcasted_iota(jnp.int32, (step, count), 0) + k
        hot = jnp.where(place == index, 1.0, 0.0).astype(bf16)
        rows = jnp.concatenate([pts_ref[:, k : k + step], str_ref[:, k : k + step]], axis=0)
        part = [nn(p, hot) for p in split(rows, 3)]
        part = part[0] + part[1] + part[2]
        total = part if total is None else total + part
    total = total.T
    each = outs[0].shape[0]
    for r, out in enumerate(outs):
        out[...] = total[r * each : (r + 1) * each]


def gather_patches(index, points, strength, walls):
    n = index.shape[1] // walls
    shape = jax.ShapeDtypeStruct((n, 2 * points.shape[0]), f32)
    return pl.pallas_call(
        patch_kernel,
        in_specs=[whole(index), whole(points), whole(strength)],
        out_specs=[whole(shape)] * walls,
        out_shape=[shape] * walls,
        name="patch_rows",
    )(index, points, strength)


def per_device(
    drop_points,
    drop_strength,
    upsample,
    base_velocity,
    near_drops,
    near_count,
    patch_points,
    patch_strength,
    wall_near,
):
    ranks = lax.axis_size("drops")
    walls = lax.axis_size("wall")
    owned, _, _ = drop_points.shape
    slots = near_drops.shape[1]
    entries = owned * slots
    depth = max(2, (entries + ranks - 1) // ranks)
    here = lax.axis_index("wall")

    targets = drop_points.transpose(1, 0, 2)

    requests, pick = make_requests(near_drops, ranks, depth)
    incoming = lax.all_to_all(requests, "drops", split_axis=0, concat_axis=0, tiled=True)
    send = gather_drops(incoming, targets, drop_strength.transpose(1, 0, 2))

    held = patch_points.shape[0]
    listed = wall_near.shape[1]
    wanted = wall_near.reshape(owned * listed)
    got = lax.all_to_all(send, "drops", split_axis=0, concat_axis=0, tiled=True)
    asked = [wanted]
    for r in range(1, walls):
        asked.append(lax.ppermute(wanted, "wall", [(w, (w + r) % walls) for w in range(walls)]))

    index = (jnp.concatenate(asked) - here * held)[None]
    rows = gather_patches(index, patch_points.T, patch_strength.T, walls)
    mine = rows[0]
    for r in range(1, walls):
        back = lax.ppermute(rows[r], "wall", [(w, (w - r) % walls) for w in range(walls)])
        mine = mine + back
    patch = mine.shape[1] // 6
    mine = mine.reshape(owned, listed, 6, patch).transpose(0, 2, 1, 3).reshape(owned, 6, -1)

    total = near_sums(near_count, pick, got, upsample, targets, base_velocity.transpose(1, 0, 2))
    total = wall_sums(mine, targets, total)
    return total.transpose(1, 0, 2)


def solution(mesh):
    return jax.shard_map(
        per_device,
        mesh=mesh,
        in_specs=(
            P(("wall", "drops"), None, None),
            P(("wall", "drops"), None, None),
            P(),
            P(("wall", "drops"), None, None),
            P(("wall", "drops"), None),
            P(("wall", "drops")),
            P("wall", None),
            P("wall", None),
            P(("wall", "drops"), None),
        ),
        out_specs=P(("wall", "drops"), None, None),
        check_vma=False,
    )
```

```python
import jax
import jax.numpy as jnp
from jax import lax
from jax.experimental import pallas as pl
from jax.experimental.pallas import tpu as pltpu
from jax.sharding import PartitionSpec as P


smoothing_square = 0.25
f32 = jnp.float32
bf16 = jnp.bfloat16


def nn(a, b):
    return jnp.dot(a, b, preferred_element_type=f32)


def split(v, count):
    out = []
    for left in reversed(range(count)):
        p = v.astype(bf16)
        out.append(p)
        if left:
            v = v - p.astype(f32)
    return out


def source_rows(row):
    y = [row(c) for c in range(3)]
    g = [row(3 + c) for c in range(3)]
    width = y[0].shape[1]
    y = [jnp.broadcast_to(v, (8, width)) for v in y]
    g = [jnp.broadcast_to(v, (8, width)) for v in g]
    at = lax.broadcasted_iota(jnp.int32, (8, width), 0)

    def lay(*values):
        out = values[-1]
        for r in range(len(values) - 2, -1, -1):
            if values[r] is not values[r + 1]:
                out = jnp.where(at <= r, values[r], out)
        return out

    one = jnp.ones((8, width), f32)
    zero = jnp.zeros((8, width), f32)
    square = y[0] * y[0] + y[1] * y[1] + y[2] * y[2]
    along = y[0] * g[0] + y[1] * g[1] + y[2] * g[2]
    grown = square + 2.0 * smoothing_square
    top = lay(g[0], g[1], g[2], g[0], g[1], g[2], g[0], g[1]) * lay(
        one, one, one, y[0], y[0], y[0], y[1], y[1]
    )
    low = lay(g[2], g[0], g[1], g[2], g[0], g[1], g[2], g[2]) * lay(
        y[1], y[2], y[2], y[2], grown, grown, grown, zero
    ) + along * lay(zero, zero, zero, zero, y[0], y[1], y[2], zero)
    c = split(jnp.concatenate([top, low], axis=0), 3)
    b = [p.astype(f32) for p in split(lay(y[0], y[1], y[2], square, y[0], y[1], y[2], square), 3)]
    first = jnp.where(at < 4, b[0], b[1])
    second = jnp.where(at < 4, b[2], one)
    dist = jnp.concatenate([first, second, first, b[0]], axis=0).astype(bf16)
    return dist, jnp.concatenate(c, axis=0), jnp.concatenate(c[:2], axis=0)


def target_rows(x):
    square = x[0] * x[0] + x[1] * x[1] + x[2] * x[2] + smoothing_square
    one = jnp.ones_like(square)
    zero = jnp.zeros_like(square)
    a = [split(-2.0 * v, 3) for v in x]
    a = [[p.astype(f32) for p in v] for v in a]
    s = [p.astype(f32) for p in split(square, 3)]
    top = [a[0][0], a[1][0], a[2][0], one]
    rows = top * 3 + s + [zero]
    rows += [a[0][1], a[1][1], a[2][1], zero] * 2
    rows += [a[0][2], a[1][2], a[2][2], zero] + [zero] * 4
    return jnp.concatenate(rows, axis=0).astype(bf16)


def finish(acc_ref, u_ref, t_ref, b_ref, o_ref, drop):
    rest = u_ref.shape[1]
    blank = jnp.zeros((128 - 3 * rest, 128), f32)
    sums = jnp.concatenate([u_ref[0], u_ref[1], u_ref[2], blank], axis=0).T
    line = jnp.sum(sums, axis=0, keepdims=True)
    q = acc_ref[0:16] + acc_ref[16:32] + acc_ref[32:48] + (acc_ref[48:64] + acc_ref[64:80])
    at = pl.ds(drop, 1)
    x = [t_ref[i, at][:, : acc_ref.shape[1]] for i in range(3)]
    square = x[0] * x[0] + x[1] * x[1] + x[2] * x[2]
    gs = [q[a : a + 1] for a in range(3)]
    h = [[q[3 + 3 * b + a : 4 + 3 * b + a] for a in range(3)] for b in range(3)]
    m = [q[12 + a : 13 + a] for a in range(3)]
    lean = x[0] * gs[0] + x[1] * gs[1] + x[2] * gs[2] - (h[0][0] + h[1][1] + h[2][2])
    for a in range(3):
        u = m[a] + square * gs[a] + x[a] * lean
        for b in range(3):
            u = u - x[b] * (2.0 * h[b][a] + h[a][b])
        u = jnp.concatenate([u, line[:, a * rest : (a + 1) * rest]], axis=1)
        o_ref[a, at] = b_ref[a, at] + u


TILE = 256


def upsample_rows(high, low, up_ref, f_ref):
    depth, fine = up_ref.shape
    rows = high.shape[0]
    ks = range(0, depth, TILE)

    def padded(v, shape):
        for axis in range(2):
            if v.shape[axis] < shape[axis]:
                gap = list(v.shape)
                gap[axis] = shape[axis] - v.shape[axis]
                v = jnp.concatenate([v, jnp.zeros(gap, v.dtype)], axis=axis)
        return v

    parts = [
        [padded(v[:, k : min(k + TILE, depth)], (rows, TILE)) for k in ks] for v in (high, low)
    ]

    def body(*accs):
        pushed = [0, 0]

        def push(m, value):
            register = pushed[m] % 2
            pushed[m] += 1
            pltpu.matmul_push_rhs(value, staging_register=register, mxu_index=m)
            return register

        tiles = list(enumerate(range(0, fine, TILE)))

        def flush(i, n0):
            n1 = min(n0 + TILE, fine)
            f = pltpu.matmul_pop(accs[i % 4])[:, : n1 - n0]
            f_ref[:, :, n0:n1] = f.reshape(f_ref.shape[0], 8, n1 - n0)

        for i, n0 in tiles:
            m = i % 2
            n1 = min(n0 + TILE, fine)
            for j, k in enumerate(ks):
                up = split(up_ref[k : min(k + TILE, depth), n0:n1], 2)
                up = [padded(p, (TILE, TILE)) for p in up]
                register = push(m, up[0])
                pltpu.matmul_acc_lhs(accs[i % 4], parts[0][j], load_staged_rhs=register)
                pltpu.matmul_acc_lhs(accs[i % 4], parts[1][j])
                register = push(m, up[1])
                pltpu.matmul_acc_lhs(accs[i % 4], parts[0][j], load_staged_rhs=register)
            if i >= 2:
                flush(*tiles[i - 2])
        for tile in tiles[-2:]:
            flush(*tile)

    pl.run_scoped(body, *[pltpu.ACC(m)((rows, TILE), f32) for m in (0, 1, 0, 1)])


def near_slot(row, width, xp_ref, acc_ref, u_ref, xb_ref, w_ref):
    whole_chunks, half = divmod(width, TILE)
    units = range(2)
    cols = {}

    def body(*refs):
        main = [refs[0:3], refs[3:6]]
        tail, high, low = refs[6:8], refs[8:10], refs[10:12]
        pushed = [0, 0]

        def push(m, value):
            register = pushed[m] % 2
            pushed[m] += 1
            pltpu.matmul_push_rhs(value, staging_register=register, mxu_index=m)
            return register

        def start(chunks):
            lhs = []
            for c in chunks:
                size = TILE if c < whole_chunks else half
                dist, three, two = source_rows(lambda r: row(r, c * TILE, size))
                cols[c] = three, two
                turned = jnp.concatenate([dist, jnp.zeros((96, size), bf16)], axis=0).T
                lhs.append(jnp.concatenate([turned, jnp.zeros((size, 128), bf16)], axis=1))
            for m in units:
                register = push(m, xp_ref[m])
                for c, value in zip(chunks, lhs):
                    into = main[m][c % 3] if c < whole_chunks else tail[m]
                    pltpu.matmul_acc_lhs(into, value, load_staged_rhs=register)
                    register = None

        def cube(c, m):
            w = lax.rsqrt(pltpu.matmul_pop(main[m][c % 3] if c < whole_chunks else tail[m]))
            return split(w * w * w, 2)

        def keep(c, m):
            hi, lo = cube(c, m)
            w_ref[c % 2, m, 0] = hi
            w_ref[c % 2, m, 1] = lo

        def reduce(c, m):
            three, two = cols[c]
            register = push(m, w_ref[c % 2, m, 0])
            pltpu.matmul_acc_lhs(high[m], three, load_staged_rhs=register)
            register = push(m, w_ref[c % 2, m, 1])
            pltpu.matmul_acc_lhs(low[m], two, load_staged_rhs=register)

        last = whole_chunks + (1 if half else 0)
        start([0])
        for c in range(whole_chunks):
            if c % 2 == 0 and c + 1 < last:
                start([k for k in (c + 1, c + 2) if k < last])
            keep(c, 0)
            if c > 0:
                reduce(c - 1, 1)
            keep(c, 1)
            reduce(c, 0)
        reduce(whole_chunks - 1, 1)
        if half:
            three, two = cols[whole_chunks]
            two = jnp.concatenate([two, jnp.zeros((16, half), bf16)], axis=0)
            both = jnp.concatenate([three, two], axis=1)
            for m in units:
                hi, lo = cube(whole_chunks, m)
                register = push(m, jnp.concatenate([hi, lo], axis=0))
                pltpu.matmul_acc_lhs(high[m], both, load_staged_rhs=register)
        for m in units:
            at = slice(m * TILE, (m + 1) * TILE)
            acc_ref[:48, at] += pltpu.matmul_pop(high[m])
            acc_ref[48:, at] += pltpu.matmul_pop(low[m])

    acc = pltpu.ACC
    pl.run_scoped(
        body,
        *[acc(m)((TILE, TILE), f32) for m in (0, 0, 0, 1, 1, 1)],
        *[acc(m)((128, TILE), f32) for m in units],
        *[acc(m)((48, TILE), f32) for m in units],
        *[acc(m)((32, TILE), f32) for m in units],
    )

    x = [xb_ref[i] for i in range(3)]
    u = [u_ref[i] for i in range(3)]
    for s0 in range(0, width, 128):
        y = [row(i, s0, 128) for i in range(3)]
        g = [row(3 + i, s0, 128) for i in range(3)]
        d = [x[i] - y[i] for i in range(3)]
        r = d[0] * d[0] + d[1] * d[1] + d[2] * d[2] + smoothing_square
        w = lax.rsqrt(r)
        w3 = w * w * w
        along = (d[0] * g[0] + d[1] * g[1] + d[2] * g[2]) * w3
        plain = (r + smoothing_square) * w3
        u = [u[i] + (plain * g[i] + along * d[i]) for i in range(3)]
    for i in range(3):
        u_ref[i] = u[i]


def set_targets(drop, t_ref, xp_ref, acc_ref, u_ref, xb_ref):
    tiled = 2 * TILE
    x = [t_ref[i, pl.ds(drop, 1)] for i in range(3)]
    feats = target_rows([v[:, :tiled] for v in x])
    for m in range(2):
        xp_ref[m, :32] = feats[:, m * TILE : (m + 1) * TILE]
    rest = xb_ref.shape[1]
    for i in range(3):
        end = jnp.concatenate([x[i][:, tiled:], jnp.zeros((1, 128 - rest), f32)], axis=1)
        xb_ref[i] = jnp.broadcast_to(end, (128, 128)).T[:rest]
    acc_ref[...] = jnp.zeros_like(acc_ref)
    u_ref[...] = jnp.zeros_like(u_ref)


def wall_kernel(wall_ref, t_ref, b_ref, o_ref, acc_ref, xp_ref, u_ref, xb_ref, w_ref):
    xp_ref[...] = jnp.zeros_like(xp_ref)

    def one_drop(drop, carry):
        set_targets(drop, t_ref, xp_ref, acc_ref, u_ref, xb_ref)
        near_slot(
            lambda c, s0, size: wall_ref[drop, c : c + 1, s0 : s0 + size],
            wall_ref.shape[2], xp_ref, acc_ref, u_ref, xb_ref, w_ref,
        )
        finish(acc_ref, u_ref, t_ref, b_ref, o_ref, drop)
        return carry

    for drop in range(t_ref.shape[1]):
        one_drop(drop, 0)


def near_kernel(
    count_ref, pick_ref, got_ref, up_ref, t_ref, b_ref, o_ref,
    cbuf, f_ref, acc_ref, xp_ref, u_ref, xb_ref, w_ref,
):
    entries = f_ref.shape[0]
    owned = t_ref.shape[1]
    slots = entries // owned
    depth = got_ref.shape[2]
    coarse = got_ref.shape[3]
    fine = up_ref.shape[1]

    @pl.when(count_ref[0] >= 0)
    def _():
        pad = jnp.zeros((2, coarse), f32)
        for e in range(entries):
            both = got_ref[pick_ref[e] // depth]
            place = pick_ref[e] % depth
            row = both[:, 0]
            for p in range(1, depth):
                row = jnp.where(place == p, both[:, p], row)
            cbuf[e] = jnp.concatenate([row, pad], axis=0)
        source = cbuf[...]
        high, low = split(source.reshape(entries * 8, coarse), 2)
        upsample_rows(high, low, up_ref, f_ref)
        tail = f_ref.shape[2] - fine - coarse
        at = lax.broadcasted_iota(jnp.int32, source.shape, 1)
        source = jnp.where(at < 3, source, -source)
        f_ref[:, :, fine:] = jnp.concatenate(
            [source, jnp.zeros((entries, 8, tail), f32)], axis=2
        )

    xp_ref[...] = jnp.zeros_like(xp_ref)

    def one_drop(drop, carry):
        set_targets(drop, t_ref, xp_ref, acc_ref, u_ref, xb_ref)

        def one_slot(slot, inner):
            entry = drop * slots + slot
            near_slot(
                lambda c, s0, size: f_ref[entry, c : c + 1, s0 : s0 + size],
                f_ref.shape[2], xp_ref, acc_ref, u_ref, xb_ref, w_ref,
            )
            return inner

        lax.fori_loop(0, count_ref[drop], one_slot, 0)
        finish(acc_ref, u_ref, t_ref, b_ref, o_ref, drop)
        return carry

    lax.fori_loop(0, owned, one_drop, 0)


def whole(a):
    zeros = (0,) * len(a.shape)
    return pl.BlockSpec(a.shape, lambda *_: zeros, pipeline_mode=pl.Buffered(1))


def sum_scratch(nodes):
    return [
        pltpu.VMEM((80, 2 * TILE), f32),
        pltpu.VMEM((2, TILE, TILE), bf16),
        pltpu.VMEM((3, nodes - 2 * TILE, 128), f32),
        pltpu.VMEM((3, nodes - 2 * TILE, 128), f32),
        pltpu.VMEM((2, 2, 2, TILE, TILE), bf16),
    ]


def wall_sums(wall, targets, base):
    return pl.pallas_call(
        wall_kernel,
        in_specs=[whole(wall), whole(targets), whole(base)],
        out_specs=whole(targets),
        scratch_shapes=sum_scratch(targets.shape[2]),
        out_shape=jax.ShapeDtypeStruct(targets.shape, f32),
        name="wall_pairs",
    )(wall, targets, base)


def near_sums(counts, pick, got, upsample, targets, base):
    nodes = targets.shape[2]
    entries = pick.shape[0]
    width = -(-(upsample.shape[1] + nodes) // 128) * 128
    smem = pl.BlockSpec(memory_space=pltpu.SMEM)
    return pl.pallas_call(
        near_kernel,
        in_specs=[smem, smem, whole(got), whole(upsample), whole(targets), whole(base)],
        out_specs=whole(targets),
        scratch_shapes=[
            pltpu.VMEM((entries, 8, nodes), f32),
            pltpu.VMEM((entries, 8, width), f32),
            *sum_scratch(nodes),
        ],
        out_shape=jax.ShapeDtypeStruct(targets.shape, f32),
        name="near_pairs",
    )(counts, pick, got, upsample, targets, base)


def request_kernel(near_ref, ask_ref, pick_ref, seen_ref):
    ranks, _, depth = ask_ref.shape
    slots, owned = near_ref.shape
    for r in range(ranks):
        seen_ref[r] = 0
        for p in range(depth):
            ask_ref[r, 0, p] = 0
    for e in range(owned * slots):
        partner = near_ref[e % slots, e // slots]
        owner = partner // owned % ranks
        place = seen_ref[owner]
        seen_ref[owner] = place + 1
        ask_ref[owner, 0, place] = partner % owned
        pick_ref[e] = owner * depth + place


def make_requests(near_drops, ranks, depth):
    slots, owned = near_drops.shape
    smem = pl.BlockSpec(memory_space=pltpu.SMEM)
    return pl.pallas_call(
        request_kernel,
        in_specs=[smem],
        out_specs=[smem, smem],
        out_shape=[
            jax.ShapeDtypeStruct((ranks, 1, depth), jnp.int32),
            jax.ShapeDtypeStruct((owned * slots,), jnp.int32),
        ],
        scratch_shapes=[pltpu.SMEM((ranks,), jnp.int32)],
        name="requests",
    )(near_drops)


def send_kernel(ask_ref, pts_ref, str_ref, o_ref):
    ranks, _, depth, _ = o_ref.shape
    for r in range(ranks):
        for p in range(depth):
            at = pl.ds(ask_ref[r, 0, p], 1)
            o_ref[r, 0:3, p : p + 1] = pts_ref[:, at]
            o_ref[r, 3:6, p : p + 1] = str_ref[:, at]


def gather_drops(incoming, points, strength):
    ranks, _, depth = incoming.shape
    shape = (ranks, 6, depth, points.shape[2])
    return pl.pallas_call(
        send_kernel,
        grid_spec=pltpu.PrefetchScalarGridSpec(
            num_scalar_prefetch=1,
            grid=(1,),
            in_specs=[whole(points), whole(strength)],
            out_specs=pl.BlockSpec(shape, lambda *_: (0,) * 4, pipeline_mode=pl.Buffered(1)),
        ),
        out_shape=jax.ShapeDtypeStruct(shape, f32),
        name="send_rows",
    )(incoming, points, strength)


def patch_kernel(index_ref, pts_ref, str_ref, *outs):
    held = pts_ref.shape[1]
    count = index_ref.shape[1]
    step = 512
    index = jnp.broadcast_to(index_ref[...], (step, count))
    total = None
    for k in range(0, held, step):
        place = lax.broadcasted_iota(jnp.int32, (step, count), 0) + k
        hot = jnp.where(place == index, 1.0, 0.0).astype(bf16)
        rows = jnp.concatenate([pts_ref[:, k : k + step], str_ref[:, k : k + step]], axis=0)
        part = [nn(p, hot) for p in split(rows, 3)]
        part = part[0] + part[1] + part[2]
        total = part if total is None else total + part
    total = total.T
    each = outs[0].shape[0]
    for r, out in enumerate(outs):
        out[...] = total[r * each : (r + 1) * each]


def gather_patches(index, points, strength, walls):
    n = index.shape[1] // walls
    shape = jax.ShapeDtypeStruct((n, 2 * points.shape[0]), f32)
    return pl.pallas_call(
        patch_kernel,
        in_specs=[whole(index), whole(points), whole(strength)],
        out_specs=[whole(shape)] * walls,
        out_shape=[shape] * walls,
        name="patch_rows",
    )(index, points, strength)


def per_device(
    drop_points,
    drop_strength,
    upsample,
    base_velocity,
    near_drops,
    near_count,
    patch_points,
    patch_strength,
    wall_near,
):
    ranks = lax.axis_size("drops")
    walls = lax.axis_size("wall")
    owned, _, _ = drop_points.shape
    slots = near_drops.shape[1]
    entries = owned * slots
    depth = max(2, (entries + ranks - 1) // ranks)
    here = lax.axis_index("wall")

    targets = drop_points.transpose(1, 0, 2)

    requests, pick = make_requests(near_drops.T, ranks, depth)
    incoming = lax.all_to_all(requests, "drops", split_axis=0, concat_axis=0, tiled=True)
    send = gather_drops(incoming, targets, drop_strength.transpose(1, 0, 2))

    held = patch_points.shape[0]
    listed = wall_near.shape[1]
    wanted = wall_near.reshape(owned * listed)
    got = lax.all_to_all(send, "drops", split_axis=0, concat_axis=0, tiled=True)
    asked = [wanted]
    for r in range(1, walls):
        asked.append(lax.ppermute(wanted, "wall", [(w, (w + r) % walls) for w in range(walls)]))

    index = (jnp.concatenate(asked) - here * held)[None]
    rows = gather_patches(index, patch_points.T, patch_strength.T, walls)
    mine = rows[0]
    for r in range(1, walls):
        back = lax.ppermute(rows[r], "wall", [(w, (w - r) % walls) for w in range(walls)])
        mine = mine + back
    patch = mine.shape[1] // 6
    mine = mine.reshape(owned, listed, 6, patch).transpose(0, 2, 1, 3).reshape(owned, 6, -1)

    total = near_sums(near_count, pick, got, upsample, targets, base_velocity.transpose(1, 0, 2))
    total = wall_sums(mine, targets, total)
    return total.transpose(1, 0, 2)


def solution(mesh):
    return jax.shard_map(
        per_device,
        mesh=mesh,
        in_specs=(
            P(("wall", "drops"), None, None),
            P(("wall", "drops"), None, None),
            P(),
            P(("wall", "drops"), None, None),
            P(("wall", "drops"), None),
            P(("wall", "drops")),
            P("wall", None),
            P("wall", None),
            P(("wall", "drops"), None),
        ),
        out_specs=P(("wall", "drops"), None, None),
        check_vma=False,
    )
```
